32 devices in a mesh: gx: 4 (over y, x), gy: 8 (over z, core).
Axes of the slice: x: 2, y: 2, z: 4, core: 2. Of those that a mesh axis runs over, the one named last changes fastest.
Arguments:
- features: bfloat16 [4, 8, 512, 128], P('gx', 'gy'), may hold values from -6 to 6
- coords: float32 [4, 8, 3, 512], P('gx', 'gy'), may hold values from 0 to 1
- migrate_x_slots: int32 [4, 8, 2, 32], P('gx', 'gy'), may hold values from 0 to 511, as said below
- migrate_y_slots: int32 [4, 8, 2, 32], P('gx', 'gy'), may hold values from 0 to 511, as said below
- ghost_slots: int32 [4, 8, 256], P('gx', 'gy'), may hold values from 0 to 511, as said below
- neighbours: int32 [4, 8, 512, 16], P('gx', 'gy'), may hold values from 0 to 2815, as said below
- source_weight: bfloat16 [128, 128], replicated, may hold values from -0.5 to 0.5
- target_weight: bfloat16 [128, 128], replicated, may hold values from -0.5 to 0.5
- radial_weight: float32 [8, 128], replicated, may hold values from -2 to 2
- environ_first: bfloat16 [128, 128], replicated, may hold values from -0.5 to 0.5
- mixing_first: bfloat16 [128, 128], replicated, may hold values from -0.5 to 0.5
- coupler_first: bfloat16 [128, 128], replicated, may hold values from -0.5 to 0.5
- environ_second: bfloat16 [128, 128], replicated, may hold values from -0.5 to 0.5
- mixing_second: bfloat16 [128, 128], replicated, may hold values from -0.5 to 0.5
- coupler_second: bfloat16 [128, 128], replicated, may hold values from -0.5 to 0.5
- readout: bfloat16 [128], replicated, may hold values from -0.5 to 0.5
Outputs:
- forces: float32 [4, 8, 3, 512], P('gx', 'gy')
- energies: float32 [4, 8, 512], P('gx', 'gy')
The draws below stay inside these ranges and needn't reach their ends.
Inputs may be any that keep to these rules, and one draw needn't show every extreme that they name: `migrate_x_slots`: in each device's two rows the 64 slots are distinct. `migrate_y_slots`: in each device's two rows the 64 slots are distinct. `ghost_slots`: each device's 256 slots are distinct. `neighbours`: an entry of atom i is either a slot of the same device other than i, or 512 + s * 256 + g with s in 0..8 but never 4 and g below 256, naming ghost g of the device at grid offset (s // 3 - 1, s % 3 - 1), periodic.
All inputs are finite; a program needn't handle non-finite values.
Results may differ from the reference program's by a relative error of at most 0.005.
Values may be sent and summed in bfloat16 or wider, within the bound.
A program may use at most 64 MiB of HBM per device.

```python
import math
import jax
import jax.numpy as jnp
from jax import lax

ATOMS_DEV = 512
GHOST_DEV = 256
MIG_DEV = 32
FEATURES = 128
CHANNELS = 128
NBASIS = 8
NBRS = 16
N_GX = 4
N_GY = 8


def pick_slots(key, picked_count):
    device_total = N_GX * N_GY
    keys = jax.random.split(key, device_total)
    full = jax.vmap(lambda one_key: jax.random.permutation(one_key, ATOMS_DEV))(keys)[:, :picked_count].astype(jnp.int32)
    inner = (jax.random.permutation(jax.random.fold_in(key, 7), ATOMS_DEV - 2) + 1).astype(jnp.int32)
    leading = jnp.concatenate([jnp.array([0, ATOMS_DEV - 1], jnp.int32), inner[:picked_count - 2]])
    return full.at[0].set(leading)


def draw_migrate_x_slots(key, part):
    chosen = pick_slots(jax.random.fold_in(key, 11), 2 * MIG_DEV)
    return chosen.reshape(N_GX, N_GY, 2, MIG_DEV)


def draw_migrate_y_slots(key, part):
    chosen = pick_slots(jax.random.fold_in(key, 13), 2 * MIG_DEV)
    return chosen.reshape(N_GX, N_GY, 2, MIG_DEV)


def draw_ghost_slots(key, part):
    chosen = pick_slots(jax.random.fold_in(key, 17), GHOST_DEV)
    return chosen.reshape(N_GX, N_GY, GHOST_DEV)


def draw_neighbours(key, part):
    shape = (N_GX, N_GY, ATOMS_DEV, NBRS)
    key_owner, key_step, key_side, key_ghost = jax.random.split(jax.random.fold_in(key, 19), 4)
    owner = jax.random.randint(key_owner, shape, 0, 2)
    stride = jax.random.randint(key_step, shape, 1, ATOMS_DEV)
    self_index = jnp.arange(ATOMS_DEV, dtype=jnp.int32)[None, None, :, None]
    local_pick = (self_index + stride) % ATOMS_DEV
    block_side = jax.random.randint(key_side, shape, 0, 8)
    block_side = block_side + (block_side >= 4).astype(jnp.int32)
    ghost_pick = jax.random.randint(key_ghost, shape, 0, GHOST_DEV)
    remote = ATOMS_DEV + block_side * GHOST_DEV + ghost_pick
    chosen = jnp.where(owner == 1, local_pick, remote).astype(jnp.int32)
    chosen = chosen.at[0, 0, 0, NBRS - 1].set(ATOMS_DEV + 9 * GHOST_DEV - 1)
    chosen = chosen.at[0, 0, 1, 0].set(0)
    return chosen


def block_levels(own_key, dims, cuts, low, top_value):
    factor_of = 1.0
    for position, parts in cuts:
        heights = jax.random.uniform(jax.random.fold_in(jax.random.fold_in(own_key, 6), position), (parts,), jnp.float32, low / len(cuts), top_value / len(cuts))
        factor_of = factor_of * jnp.repeat(jnp.exp(heights), dims[position] // parts).reshape((-1,) + (1,) * (len(dims) - 1 - position))
    return factor_of


def centred(rng, dims, width, most, shards=(), held_as=jnp.bfloat16):
    result = jax.random.normal(rng, dims, jnp.float32) * width
    if len(shards) > 0:
        result = block_levels(rng, dims, shards, -0.22, 0.18) * result
    return jnp.clip(result, min=-most, max=most).astype(held_as)


def setup_inputs(seed: int = 0) -> dict:
    streams_of = jax.random.split(jax.random.key(seed), 17)
    features = centred(streams_of[0], (N_GX, N_GY, ATOMS_DEV, FEATURES), 1.0, 6.0, ((0, 4), (1, 8)))
    coords = jnp.clip(1.0 * jax.random.uniform(streams_of[1], (N_GX, N_GY, 3, ATOMS_DEV), jnp.float32) ** block_levels(streams_of[1], (N_GX, N_GY, 3, ATOMS_DEV), ((0, 4), (1, 8)), -0.2, 0.2), 0.0, 1.0)
    migrate_x_slots = draw_migrate_x_slots(jax.random.fold_in(streams_of[16], 71), 0)
    migrate_y_slots = draw_migrate_y_slots(jax.random.fold_in(streams_of[16], 71), 0)
    ghost_slots = draw_ghost_slots(jax.random.fold_in(streams_of[16], 71), 0)
    neighbours = draw_neighbours(jax.random.fold_in(streams_of[16], 71), 0)
    source_weight = centred(streams_of[6], (FEATURES, CHANNELS), FEATURES ** -0.5, 0.5)
    target_weight = centred(streams_of[7], (FEATURES, CHANNELS), FEATURES ** -0.5, 0.5)
    radial_weight = centred(streams_of[8], (NBASIS, CHANNELS), NBASIS ** -0.5, 2.0, (), jnp.float32)
    environ_first = centred(streams_of[9], (CHANNELS, CHANNELS), CHANNELS ** -0.5, 0.5)
    mixing_first = centred(streams_of[10], (CHANNELS, CHANNELS), CHANNELS ** -0.5, 0.5)
    coupler_first = centred(streams_of[11], (CHANNELS, CHANNELS), CHANNELS ** -0.5, 0.5)
    environ_second = centred(streams_of[12], (CHANNELS, CHANNELS), CHANNELS ** -0.5, 0.5)
    mixing_second = centred(streams_of[13], (CHANNELS, CHANNELS), CHANNELS ** -0.5, 0.5)
    coupler_second = centred(streams_of[14], (CHANNELS, CHANNELS), CHANNELS ** -0.5, 0.5)
    readout = centred(streams_of[15], (CHANNELS,), CHANNELS ** -0.5, 0.5)
    return dict(features=features, coords=coords, migrate_x_slots=migrate_x_slots, migrate_y_slots=migrate_y_slots, ghost_slots=ghost_slots, neighbours=neighbours, source_weight=source_weight, target_weight=target_weight, radial_weight=radial_weight, environ_first=environ_first, mixing_first=mixing_first, coupler_first=coupler_first, environ_second=environ_second, mixing_second=mixing_second, coupler_second=coupler_second, readout=readout)


soften = 0.25
cutoff = 2.0

def block_energy(positions, first_row, neighbour_block, source_block, target_table, radial_weight, layers, readout):
    block_rows, slots_per = neighbour_block.shape
    breadth = target_table.shape[1]
    flat_index = neighbour_block.reshape(block_rows * slots_per)
    pos_own = lax.dynamic_slice_in_dim(positions, first_row, block_rows, 1)
    pos_far = jnp.take(positions, flat_index, axis=1).reshape(3, block_rows, slots_per)
    offset = pos_far - pos_own[:, :, None]
    length = jnp.sqrt(lax.optimization_barrier(jnp.sum(offset * offset, axis=0)) + soften)
    direction = offset / length[None]
    scaled = length / cutoff
    smooth = (1.0 - scaled * scaled) ** 2
    frequency = (jnp.arange(radial_weight.shape[0]) + 1).astype(jnp.float32) * math.pi
    bessel = jnp.sin(scaled[:, :, None] * frequency) / length[:, :, None] * smooth[:, :, None]
    radial = jnp.einsum('rnb,bc->rnc', bessel, radial_weight, precision=lax.Precision.HIGHEST)
    gathered = jnp.take(target_table, flat_index, axis=0).reshape(block_rows, slots_per, breadth)
    paired = source_block.astype(jnp.float32)[:, None, :] + gathered.astype(jnp.float32) + radial
    hidden = jax.nn.silu(paired).reshape(block_rows * slots_per, breadth).astype(jnp.bfloat16)
    weighted = direction * smooth[None]
    norm_scale = 1.0 / math.sqrt(slots_per)
    latent = None
    for environ, mixing, coupler in layers:
        carried = jnp.dot(hidden, environ, preferred_element_type=jnp.float32).reshape(block_rows, slots_per, breadth)
        environment = [lax.optimization_barrier(jnp.sum(weighted[k][:, :, None] * carried, axis=1)) for k in range(3)]
        coupled = direction[0][:, :, None] * environment[0][:, None, :]
        coupled = coupled + direction[1][:, :, None] * environment[1][:, None, :]
        coupled = coupled + direction[2][:, :, None] * environment[2][:, None, :]
        coupled = (coupled * norm_scale).reshape(block_rows * slots_per, breadth).astype(jnp.bfloat16)
        mixed = jnp.dot(hidden, mixing, preferred_element_type=jnp.float32) + jnp.dot(coupled, coupler, preferred_element_type=jnp.float32)
        latent = jax.nn.silu(mixed)
        hidden = latent.astype(jnp.bfloat16)
    edge_energy = lax.optimization_barrier(jnp.sum(latent * readout.astype(jnp.float32)[None, :], axis=1)).reshape(block_rows, slots_per) * smooth
    atom_energy = lax.optimization_barrier(jnp.sum(edge_energy, axis=1))
    return (jnp.sum(atom_energy), atom_energy)

def device_forces(positions, neighbours, source_rows, target_table, radial_weight, layers, readout):
    atom_count = neighbours.shape[0]
    block_atoms = math.gcd(atom_count, 256)
    block_count = atom_count // block_atoms

    def advance(total, block_number):
        first_row = block_number * block_atoms
        neighbour_block = lax.dynamic_slice_in_dim(neighbours, first_row, block_atoms, 0)
        source_block = lax.dynamic_slice_in_dim(source_rows, first_row, block_atoms, 0)

        def energy_of(table_pos):
            return block_energy(table_pos, first_row, neighbour_block, source_block, target_table, radial_weight, layers, readout)
        gradient, atom_energy = jax.grad(energy_of, has_aux=True)(positions)
        return (total + gradient, atom_energy)
    total, energies = lax.scan(advance, jnp.zeros(positions.shape, jnp.float32), jnp.arange(block_count, dtype=jnp.int32))
    return (total, energies.reshape(atom_count))

def take_rows(table, picks):
    return table[picks]

def take_columns(table, picks):
    return table[:, picks]

def put_rows(table, picks, values):
    return table.at[picks].set(values)

def put_columns(table, picks, values):
    return table.at[:, picks].set(values)

def add_columns(table, picks, values):
    return table.at[:, picks].add(values)

def migrate(features, coords, slots, axis_number):
    grid_take_rows = jax.vmap(jax.vmap(take_rows))
    grid_take_cols = jax.vmap(jax.vmap(take_columns))
    grid_put_rows = jax.vmap(jax.vmap(put_rows))
    grid_put_cols = jax.vmap(jax.vmap(put_columns))
    plus_rows = grid_take_rows(features, slots[:, :, 0])
    minus_rows = grid_take_rows(features, slots[:, :, 1])
    plus_cols = grid_take_cols(coords, slots[:, :, 0])
    minus_cols = grid_take_cols(coords, slots[:, :, 1])
    features = grid_put_rows(features, slots[:, :, 0], jnp.roll(plus_rows, 1, axis=axis_number))
    features = grid_put_rows(features, slots[:, :, 1], jnp.roll(minus_rows, -1, axis=axis_number))
    coords = grid_put_cols(coords, slots[:, :, 0], jnp.roll(plus_cols, 1, axis=axis_number))
    coords = grid_put_cols(coords, slots[:, :, 1], jnp.roll(minus_cols, -1, axis=axis_number))
    return (features, coords)

def reference(features, coords, migrate_x_slots, migrate_y_slots, ghost_slots, neighbours, source_weight, target_weight, radial_weight, environ_first, mixing_first, coupler_first, environ_second, mixing_second, coupler_second, readout):
    features, coords = migrate(features, coords, migrate_x_slots, 0)
    features, coords = migrate(features, coords, migrate_y_slots, 1)
    ghost_rows = jax.vmap(jax.vmap(take_rows))(features, ghost_slots)
    ghost_coords = jax.vmap(jax.vmap(take_columns))(coords, ghost_slots)
    layers = ((environ_first, mixing_first, coupler_first), (environ_second, mixing_second, coupler_second))
    atom_count = features.shape[2]
    ghost_count = ghost_slots.shape[2]

    def one_device(flat_id):
        grid_x = flat_id // N_GY
        grid_y = flat_id % N_GY
        own_rows = features[grid_x, grid_y]
        own_coords = coords[grid_x, grid_y]
        row_parts = [own_rows]
        coord_parts = [own_coords]
        for shift_a in range(3):
            for shift_b in range(3):
                near_x = (grid_x + shift_a - 1 + N_GX) % N_GX
                near_y = (grid_y + shift_b - 1 + N_GY) % N_GY
                row_parts.append(ghost_rows[near_x, near_y])
                coord_parts.append(ghost_coords[near_x, near_y])
        table_rows = jnp.concatenate(row_parts, axis=0)
        positions = jnp.concatenate(coord_parts, axis=1)
        source_rows = jnp.dot(own_rows, source_weight, preferred_element_type=jnp.float32).astype(jnp.bfloat16)
        target_table = jnp.dot(table_rows, target_weight, preferred_element_type=jnp.float32).astype(jnp.bfloat16)
        return device_forces(positions, neighbours[grid_x, grid_y], source_rows, target_table, radial_weight, layers, readout)
    gradients, energies = lax.map(one_device, jnp.arange(N_GX * N_GY, dtype=jnp.int32))
    gradients = gradients.reshape(N_GX, N_GY, 3, atom_count + 9 * ghost_count)
    local_part = gradients[:, :, :, :atom_count]
    ghost_part = gradients[:, :, :, atom_count:].reshape(N_GX, N_GY, 3, 3, 3, ghost_count)
    returned = jnp.zeros((N_GX, N_GY, 3, ghost_count), jnp.float32)
    for shift_a in range(3):
        for shift_b in range(3):
            returned = returned + jnp.roll(ghost_part[:, :, :, shift_a, shift_b], (shift_a - 1, shift_b - 1), axis=(0, 1))
    total = jax.vmap(jax.vmap(add_columns))(local_part, ghost_slots, returned)
    return (-total, energies.reshape(N_GX, N_GY, atom_count))
```

```python
import functools
import math

import jax
import jax.numpy as jnp
from jax import lax
from jax.experimental import pallas as pl
from jax.experimental.pallas import tpu as pltpu
from jax.sharding import PartitionSpec as P

soften = 0.25
cutoff = 2.0


def from_behind(value, axis, steps):
    count = lax.axis_size(axis)
    pairs = [(source, (source + steps) % count) for source in range(count)]
    return lax.ppermute(value, axis, pairs)


def extended(shard, sides, width):
    for axis, dim in sides:
        count, length = (lax.axis_size(axis), shard.shape[dim])
        up = [(i, (i + 1) % count) for i in range(count)]
        down = [(j, i) for i, j in up]
        last = lax.slice_in_dim(shard, length - width, length, axis=dim)
        first = lax.slice_in_dim(shard, 0, width, axis=dim)
        before = lax.ppermute(last, axis, up)
        after = lax.ppermute(first, axis, down)
        shard = jnp.concatenate([before, shard, after], axis=dim)
    return shard


def split_three(value):
    top = value.astype(jnp.bfloat16).astype(jnp.float32)
    rest = value - top
    middle = rest.astype(jnp.bfloat16).astype(jnp.float32)
    return (top, middle, rest - middle)


def sigmoid(value):
    return 0.5 * jnp.tanh(0.5 * value) + 0.5


def turned(weight):
    return weight.astype(jnp.float32).T.astype(jnp.bfloat16)


def edge_kernel(
    block_atoms,
    index_smem,
    index_ref,
    table_ref,
    source_ref,
    place_ref,
    own_ref,
    radial_ref,
    environ_first,
    mixing_first,
    coupler_first,
    environ_second,
    mixing_second,
    coupler_second,
    readout_ref,
    scatter_ref,
    atom_ref,
    gathered,
    scalars,
    results,
    saved,
    forward_weights,
    backward_weights,
    environ_turned,
    radial_in,
    radial_out,
    pick_weights,
    place_split,
):
    slots_per, _, atom_count = index_ref.shape
    breadth = table_ref.shape[1]
    groups = place_ref.shape[1]
    f32 = jnp.float32
    bf16 = jnp.bfloat16
    step = 16

    @pl.loop(0, slots_per)
    def _(slot):
        @pl.loop(0, atom_count // step)
        def _(part):
            base = pl.multiple_of(part * step, step)
            for u in range(step):
                row = index_smem[slot * atom_count + base + u]
                gathered[slot, pl.ds(base + u, 1), :] = table_ref[pl.ds(row, 1), :]

    forward_weights[0, :, :breadth] = environ_first[...]
    forward_weights[0, :, breadth:] = mixing_first[...]
    forward_weights[1, :, :breadth] = environ_second[...]
    forward_weights[1, :, breadth:] = mixing_second[...]
    backward_weights[0, :, :breadth] = turned(coupler_first[...])
    backward_weights[0, :, breadth:] = turned(mixing_first[...])
    backward_weights[1, :, :breadth] = turned(coupler_second[...])
    backward_weights[1, :, breadth:] = turned(mixing_second[...])
    environ_turned[0] = turned(environ_first[...])
    environ_turned[1] = turned(environ_second[...])
    w_top, w_mid, w_low = split_three(radial_ref[...])
    basis = radial_ref.shape[0]
    lead = jnp.zeros((8, breadth), f32)
    tail = jnp.zeros((breadth - 8 - 6 * basis, breadth), f32)
    radial_in[...] = jnp.concatenate(
        [lead, w_top, w_mid, w_low, w_top, w_mid, w_top, tail], axis=0
    ).astype(bf16)
    wide = jnp.concatenate(
        [lead, w_top, w_mid, jnp.zeros((breadth - 8 - 2 * basis, breadth), f32)], axis=0
    ).T.astype(bf16)
    radial_out[:breadth, :] = wide
    radial_out[breadth:, :] = wide
    lane_id = lax.broadcasted_iota(jnp.int32, (breadth, breadth), 1)
    for k in range(4):
        pick_weights[k * breadth : (k + 1) * breadth, :] = (
            jnp.where(lane_id == k, 1.0, 0.0).astype(bf16)
        )
    places = place_ref[...].reshape(3 * groups, breadth)
    p_top, p_mid, p_low = split_three(places)
    place_split[...] = jnp.concatenate([p_top, p_mid, p_low], axis=0).astype(bf16)

    def chosen(slot):
        index = index_ref[slot]
        low = lax.rem(index, breadth)
        high = lax.div(index, breadth)
        rows = lax.broadcasted_iota(jnp.int32, (breadth, atom_count), 0)
        one_hot = jnp.where(rows == low, 1.0, 0.0).astype(bf16)
        group_rows = lax.broadcasted_iota(jnp.int32, (groups, atom_count), 0)
        return (one_hot, group_rows == high)

    @pl.loop(0, slots_per)
    def _(slot):
        one_hot, in_group = chosen(slot)
        found = jnp.dot(place_split[...], one_hot, preferred_element_type=f32)
        size = 3 * groups
        found = found[:size] + found[size : 2 * size] + found[2 * size :]
        offsets = []
        for k in range(3):
            far = jnp.sum(
                jnp.where(in_group, found[k * groups : (k + 1) * groups], 0.0),
                axis=0,
                keepdims=True,
            )
            offsets.append(far - own_ref[k : k + 1, :])
        square = offsets[0] * offsets[0] + offsets[1] * offsets[1] + offsets[2] * offsets[2]
        length = jnp.sqrt(square + soften)
        inverse = 1.0 / length
        scaled = length / cutoff
        smooth = (1.0 - scaled * scaled) ** 2
        angle = scaled * math.pi
        sine = jnp.sin(angle)
        cosine = jnp.cos(angle)
        factor = inverse * smooth
        before, now = (jnp.zeros_like(sine), sine)
        waves = []
        for _ in range(basis):
            waves.append(now * factor)
            before, now = (now, 2.0 * cosine * now - before)
        bessel = jnp.concatenate(waves, axis=0)
        b_top, b_mid, b_low = split_three(bessel)
        blank = jnp.zeros_like(sine)
        head = [offsets[k] * inverse for k in range(3)] + [smooth] + [blank] * 4
        spare = jnp.zeros((breadth - 8 - 6 * basis, atom_count), f32)
        stack = jnp.concatenate(
            head + [b_top, b_top, b_top, b_mid, b_mid, b_low, spare], axis=0
        )
        scalars[slot] = stack.T
        saved[slot] = jnp.concatenate(offsets + [length, sine, cosine, blank, blank], axis=0)

    norm_scale = 1.0 / math.sqrt(slots_per)
    edges = slots_per * block_atoms
    cube = (slots_per, block_atoms, breadth)
    readout_row = readout_ref[...].astype(f32)[None]
    couplers = (coupler_first, coupler_second)
    ee_lane = lax.broadcasted_iota(jnp.int32, (edges, breadth), 1) == 4

    def product(left, right):
        return jnp.dot(left.astype(bf16), right, preferred_element_type=f32)

    @pl.loop(0, atom_count // block_atoms)
    def _(block):
        first = pl.multiple_of(block * block_atoms, block_atoms)
        atoms = pl.ds(first, block_atoms)
        narrow = scalars[:, atoms, :]
        radial = product(narrow.reshape(edges, breadth), radial_in[...]).reshape(cube)
        paired = gathered[:, atoms, :] + source_ref[atoms, :][None] + radial
        gate = sigmoid(paired)
        value = paired * gate
        slopes = [gate + value * (1.0 - gate)]
        hidden = value.reshape(edges, breadth).astype(bf16)
        direction = [jnp.broadcast_to(narrow[:, :, k : k + 1], cube) for k in range(3)]
        smooth = jnp.broadcast_to(narrow[:, :, 3:4], cube)
        kept = []
        for layer in range(2):
            both = jnp.dot(hidden, forward_weights[layer], preferred_element_type=f32)
            carried = both[:, :breadth].reshape(cube)
            eased = smooth * carried
            environment = [
                jnp.sum(direction[k] * eased, axis=0) * norm_scale for k in range(3)
            ]
            coupled = direction[0] * environment[0][None]
            coupled = coupled + direction[1] * environment[1][None]
            coupled = coupled + direction[2] * environment[2][None]
            mixed = both[:, breadth:] + product(
                coupled.reshape(edges, breadth), couplers[layer][...]
            )
            mixed = mixed.reshape(cube)
            gate = sigmoid(mixed)
            value = mixed * gate
            slopes.append(gate + value * (1.0 - gate))
            kept.append((carried, eased, environment))
            if layer == 0:
                hidden = value.reshape(edges, breadth).astype(bf16)
        edge_energy = jnp.sum(value * readout_row, axis=2, keepdims=True)
        flow = smooth * readout_row
        sums = None
        for layer in (1, 0):
            carried, eased, environment = kept[layer]
            mixed_grad = flow * slopes[layer + 1]
            back = product(mixed_grad.reshape(edges, breadth), backward_weights[layer])
            coupled_grad = back[:, :breadth].reshape(cube)
            environment_grad = [
                jnp.sum(direction[k] * coupled_grad, axis=0) * norm_scale for k in range(3)
            ]
            spread = direction[0] * environment_grad[0][None]
            spread = spread + direction[1] * environment_grad[1][None]
            spread = spread + direction[2] * environment_grad[2][None]
            parts = [
                coupled_grad * environment[k][None] + eased * environment_grad[k][None]
                for k in range(3)
            ] + [carried * spread]
            sums = parts if sums is None else [x + y for x, y in zip(sums, parts)]
            flow = back[:, breadth:].reshape(cube) + product(
                (smooth * spread).reshape(edges, breadth), environ_turned[layer]
            ).reshape(cube)
        paired_grad = (flow * slopes[0]).reshape(edges, breadth)
        high = paired_grad.astype(bf16)
        low = (paired_grad - high.astype(f32)).astype(bf16)
        total = jnp.dot(
            jnp.concatenate([high, low], axis=1), radial_out[...], preferred_element_type=f32
        )
        total = total + jnp.dot(
            jnp.concatenate([x.reshape(edges, breadth).astype(bf16) for x in sums], axis=1),
            pick_weights[...],
            preferred_element_type=f32,
        )
        total = jnp.where(
            ee_lane, jnp.broadcast_to(edge_energy, cube).reshape(edges, breadth), total
        )
        results[:, atoms, :] = total.reshape(cube)

    scatter_ref[...] = jnp.zeros(scatter_ref.shape, f32)
    atom_ref[...] = jnp.zeros(atom_ref.shape, f32)

    @pl.loop(0, slots_per)
    def _(slot):
        flat = results[slot].T
        data = saved[slot]
        offsets = [data[k : k + 1] for k in range(3)]
        length, sine, cosine = (data[3:4], data[4:5], data[5:6])
        inverse = 1.0 / length
        scaled = length / cutoff
        under = 1.0 - scaled * scaled
        smooth = under * under
        direction = [offsets[k] * inverse for k in range(3)]
        sin_before, sin_now = (jnp.zeros_like(sine), sine)
        cos_before, cos_now = (jnp.ones_like(sine), cosine)
        first_sum = jnp.zeros_like(sine)
        second_sum = jnp.zeros_like(sine)
        for b in range(basis):
            grad = flat[8 + b : 9 + b] + flat[8 + basis + b : 9 + basis + b]
            first_sum = first_sum + grad * sin_now
            second_sum = second_sum + grad * (cos_now * ((b + 1) * math.pi / cutoff))
            sin_before, sin_now = (sin_now, 2.0 * cosine * sin_now - sin_before)
            cos_before, cos_now = (cos_now, 2.0 * cosine * cos_now - cos_before)
        edge_energy = flat[4:5]
        smooth_grad = flat[3:4] + edge_energy + first_sum * inverse
        along = flat[0:1] * direction[0] + flat[1:2] * direction[1] + flat[2:3] * direction[2]
        length_grad = smooth * inverse * (second_sum - first_sum * inverse)
        length_grad = length_grad - smooth_grad * under * (2.0 * scaled / cutoff) * 2.0
        length_grad = length_grad - along * inverse
        one_hot, in_group = chosen(slot)
        pieces = []
        atom_rows = []
        for k in range(3):
            grad = flat[k : k + 1] * inverse + length_grad * direction[k]
            atom_rows.append(-grad)
            pieces.append(jnp.where(in_group, jnp.broadcast_to(grad, in_group.shape), 0.0))
        spread = jnp.concatenate(pieces, axis=0)
        top = spread.astype(bf16)
        low = (spread - top.astype(f32)).astype(bf16)
        for piece in (top, low):
            scatter_ref[...] += lax.dot_general(
                piece, one_hot, (((1,), (1,)), ((), ())), preferred_element_type=f32
            )
        blank = jnp.zeros_like(sine)
        atom_rows = atom_rows + [edge_energy * smooth] + [blank] * 4
        atom_ref[...] += jnp.concatenate(atom_rows, axis=0)


def device_forces(positions, neighbours, source_rows, target_table, radial_weight, layers, readout):
    atom_count, slots_per = neighbours.shape
    total_rows, breadth = target_table.shape
    basis = radial_weight.shape[0]
    groups = -(-total_rows // breadth)
    groups = -(-groups // 8) * 8
    by_slot = neighbours.T
    places = jnp.pad(positions, ((0, 0), (0, groups * breadth - total_rows)))
    places = places.reshape(3, groups, breadth)
    own = jnp.pad(positions[:, :atom_count], ((0, 5), (0, 0)))
    weights = [w for layer in layers for w in layer]
    f32 = jnp.float32
    bf16 = jnp.bfloat16
    vmem = pl.BlockSpec(memory_space=pltpu.VMEM)
    smem = pl.BlockSpec(memory_space=pltpu.SMEM)
    block_atoms = math.gcd(atom_count, 16)
    cube = (slots_per, atom_count, breadth)
    scattered, by_atom = pl.pallas_call(
        functools.partial(edge_kernel, block_atoms),
        out_shape=(
            jax.ShapeDtypeStruct((3 * groups, breadth), f32),
            jax.ShapeDtypeStruct((8, atom_count), f32),
        ),
        in_specs=[smem] + [vmem] * 13,
        out_specs=(vmem, vmem),
        scratch_shapes=[
            pltpu.VMEM(cube, f32),
            pltpu.VMEM(cube, f32),
            pltpu.VMEM(cube, f32),
            pltpu.VMEM((slots_per, 8, atom_count), f32),
            pltpu.VMEM((2, breadth, 2 * breadth), bf16),
            pltpu.VMEM((2, breadth, 2 * breadth), bf16),
            pltpu.VMEM((2, breadth, breadth), bf16),
            pltpu.VMEM((breadth, breadth), bf16),
            pltpu.VMEM((2 * breadth, breadth), bf16),
            pltpu.VMEM((4 * breadth, breadth), bf16),
            pltpu.VMEM((9 * groups, breadth), bf16),
        ],
        compiler_params=pltpu.CompilerParams(vmem_limit_bytes=48 * 1024 * 1024),
        name="edges",
    )(
        by_slot.reshape(-1),
        by_slot[:, None, :],
        target_table.astype(f32),
        source_rows.astype(f32),
        places,
        own,
        radial_weight,
        *weights,
        readout[None],
    )
    gradient = scattered.reshape(3, groups * breadth)[:, :total_rows]
    own_part = gradient[:, :atom_count] + by_atom[:3]
    gradient = jnp.concatenate([own_part, gradient[:, atom_count:]], axis=1)
    return (gradient, by_atom[3])


def move_along_x(own_rows, own_coords, slots):
    for column, stride in ((0, 1), (1, -1)):
        picked = slots[column]
        arrived_rows = from_behind(own_rows[picked], "gx", stride)
        arrived_coords = from_behind(own_coords[:, picked], "gx", stride)
        own_rows = own_rows.at[picked].set(arrived_rows)
        own_coords = own_coords.at[:, picked].set(arrived_coords)
    return (own_rows, own_coords)


def move_along_y(own_rows, own_coords, slots):
    for column, stride in ((0, 1), (1, -1)):
        picked = slots[column]
        arrived_rows = from_behind(own_rows[picked], "gy", stride)
        arrived_coords = from_behind(own_coords[:, picked], "gy", stride)
        own_rows = own_rows.at[picked].set(arrived_rows)
        own_coords = own_coords.at[:, picked].set(arrived_coords)
    return (own_rows, own_coords)


def fold_back(ghost_grad):
    partial_sum = ghost_grad[:, :, 1]
    for column, stride in ((0, -1), (2, 1)):
        partial_sum = partial_sum + from_behind(ghost_grad[:, :, column], "gy", stride)
    whole = partial_sum[:, 1]
    for column, stride in ((0, -1), (2, 1)):
        whole = whole + from_behind(partial_sum[:, column], "gx", stride)
    return whole


def per_device(
    features,
    coords,
    migrate_x_slots,
    migrate_y_slots,
    ghost_slots,
    neighbours,
    source_weight,
    target_weight,
    radial_weight,
    environ_first,
    mixing_first,
    coupler_first,
    environ_second,
    mixing_second,
    coupler_second,
    readout,
):
    own_rows = features[0, 0]
    own_coords = coords[0, 0]
    own_rows, own_coords = move_along_x(own_rows, own_coords, migrate_x_slots[0, 0])
    own_rows, own_coords = move_along_y(own_rows, own_coords, migrate_y_slots[0, 0])
    atom_count = own_rows.shape[0]
    ghosts = ghost_slots[0, 0]
    ghost_count = ghosts.shape[0]
    ghost_coords = own_coords[:, ghosts]
    source_rows = jnp.dot(own_rows, source_weight, preferred_element_type=jnp.float32).astype(
        jnp.bfloat16
    )
    payload = own_rows[ghosts]
    breadth = payload.shape[1]
    halo_rows = extended(payload[None, None], (("gx", 0), ("gy", 1)), 1)
    halo_coords = extended(ghost_coords[None, None], (("gx", 0), ("gy", 1)), 1)
    stacked = jnp.concatenate([own_rows, halo_rows.reshape(9 * ghost_count, breadth)], axis=0)
    target_table = jnp.dot(stacked, target_weight, preferred_element_type=jnp.float32).astype(
        jnp.bfloat16
    )
    positions = jnp.concatenate(
        [own_coords, jnp.moveaxis(halo_coords, 2, 0).reshape(3, 9 * ghost_count)], axis=1
    )
    layers = (
        (environ_first, mixing_first, coupler_first),
        (environ_second, mixing_second, coupler_second),
    )
    gradient, energies = device_forces(
        positions, neighbours[0, 0], source_rows, target_table, radial_weight, layers, readout
    )
    returned = fold_back(gradient[:, atom_count:].reshape(3, 3, 3, ghost_count))
    total = gradient[:, :atom_count].at[:, ghosts].add(returned)
    return ((-total)[None, None], energies[None, None])


def solution(mesh):
    in_specs = (
        P("gx", "gy", None, None),
        P("gx", "gy", None, None),
        P("gx", "gy", None, None),
        P("gx", "gy", None, None),
        P("gx", "gy", None),
        P("gx", "gy", None, None),
        P(),
        P(),
        P(),
        P(),
        P(),
        P(),
        P(),
        P(),
        P(),
        P(),
    )
    out_specs = (P("gx", "gy", None, None), P("gx", "gy", None))
    return jax.shard_map(
        per_device, mesh=mesh, in_specs=in_specs, out_specs=out_specs, check_vma=False
    )
```

```python
import functools
import math

import jax
import jax.numpy as jnp
from jax import lax
from jax.experimental import pallas as pl
from jax.experimental.pallas import tpu as pltpu
from jax.sharding import PartitionSpec as P

soften = 0.25
cutoff = 2.0


def split_three(value):
    top = value.astype(jnp.bfloat16).astype(jnp.float32)
    rest = value - top
    middle = rest.astype(jnp.bfloat16).astype(jnp.float32)
    return (top, middle, rest - middle)


def sigmoid(value):
    return 0.5 * jnp.tanh(0.5 * value) + 0.5


def turned(weight):
    return weight.astype(jnp.float32).T.astype(jnp.bfloat16)


def edge_kernel(
    block_atoms,
    index_smem,
    index_ref,
    table_ref,
    source_ref,
    place_ref,
    own_ref,
    radial_ref,
    environ_first,
    mixing_first,
    coupler_first,
    environ_second,
    mixing_second,
    coupler_second,
    readout_ref,
    scatter_ref,
    atom_ref,
    gathered,
    scalars,
    results,
    saved,
    forward_weights,
    backward_weights,
    environ_turned,
    radial_in,
    radial_out,
    pick_weights,
    place_split,
):
    slots_per, _, atom_count = index_ref.shape
    breadth = table_ref.shape[1]
    groups = place_ref.shape[1]
    f32 = jnp.float32
    bf16 = jnp.bfloat16
    step = 16

    @pl.loop(0, slots_per)
    def _(slot):
        @pl.loop(0, atom_count // step)
        def _(part):
            base = pl.multiple_of(part * step, step)
            for u in range(step):
                row = index_smem[slot * atom_count + base + u]
                gathered[slot, pl.ds(base + u, 1), :] = table_ref[pl.ds(row, 1), :]

    forward_weights[0, :, :breadth] = environ_first[...]
    forward_weights[0, :, breadth:] = mixing_first[...]
    forward_weights[1, :, :breadth] = environ_second[...]
    forward_weights[1, :, breadth:] = mixing_second[...]
    backward_weights[0, :, :breadth] = turned(coupler_first[...])
    backward_weights[0, :, breadth:] = turned(mixing_first[...])
    backward_weights[1, :, :breadth] = turned(coupler_second[...])
    backward_weights[1, :, breadth:] = turned(mixing_second[...])
    environ_turned[0] = turned(environ_first[...])
    environ_turned[1] = turned(environ_second[...])
    w_top, w_mid, w_low = split_three(radial_ref[...])
    basis = radial_ref.shape[0]
    lead = jnp.zeros((8, breadth), f32)
    tail = jnp.zeros((breadth - 8 - 6 * basis, breadth), f32)
    radial_in[...] = jnp.concatenate(
        [lead, w_top, w_mid, w_low, w_top, w_mid, w_top, tail], axis=0
    ).astype(bf16)
    wide = jnp.concatenate(
        [lead, w_top, w_mid, jnp.zeros((breadth - 8 - 2 * basis, breadth), f32)], axis=0
    ).T.astype(bf16)
    radial_out[:breadth, :] = wide
    radial_out[breadth:, :] = wide
    lane_id = lax.broadcasted_iota(jnp.int32, (breadth, breadth), 1)
    for k in range(4):
        pick_weights[k * breadth : (k + 1) * breadth, :] = (
            jnp.where(lane_id == k, 1.0, 0.0).astype(bf16)
        )
    places = place_ref[...].reshape(3 * groups, breadth)
    p_top, p_mid, p_low = split_three(places)
    place_split[...] = jnp.concatenate([p_top, p_mid, p_low], axis=0).astype(bf16)

    def chosen(slot):
        index = index_ref[slot]
        low = lax.rem(index, breadth)
        high = lax.div(index, breadth)
        rows = lax.broadcasted_iota(jnp.int32, (breadth, atom_count), 0)
        one_hot = jnp.where(rows == low, 1.0, 0.0).astype(bf16)
        group_rows = lax.broadcasted_iota(jnp.int32, (groups, atom_count), 0)
        return (one_hot, group_rows == high)

    @pl.loop(0, slots_per)
    def _(slot):
        one_hot, in_group = chosen(slot)
        found = jnp.dot(place_split[...], one_hot, preferred_element_type=f32)
        size = 3 * groups
        found = found[:size] + found[size : 2 * size] + found[2 * size :]
        offsets = []
        for k in range(3):
            far = jnp.sum(
                jnp.where(in_group, found[k * groups : (k + 1) * groups], 0.0),
                axis=0,
                keepdims=True,
            )
            offsets.append(far - own_ref[k : k + 1, :])
        square = offsets[0] * offsets[0] + offsets[1] * offsets[1] + offsets[2] * offsets[2]
        length = jnp.sqrt(square + soften)
        inverse = 1.0 / length
        scaled = length / cutoff
        smooth = (1.0 - scaled * scaled) ** 2
        angle = scaled * math.pi
        sine = jnp.sin(angle)
        cosine = jnp.cos(angle)
        factor = inverse * smooth
        before, now = (jnp.zeros_like(sine), sine)
        waves = []
        for _ in range(basis):
            waves.append(now * factor)
            before, now = (now, 2.0 * cosine * now - before)
        bessel = jnp.concatenate(waves, axis=0)
        b_top, b_mid, b_low = split_three(bessel)
        blank = jnp.zeros_like(sine)
        head = [offsets[k] * inverse for k in range(3)] + [smooth] + [blank] * 4
        spare = jnp.zeros((breadth - 8 - 6 * basis, atom_count), f32)
        stack = jnp.concatenate(
            head + [b_top, b_top, b_top, b_mid, b_mid, b_low, spare], axis=0
        )
        scalars[slot] = stack.T
        saved[slot] = jnp.concatenate(offsets + [length, sine, cosine, blank, blank], axis=0)

    norm_scale = 1.0 / math.sqrt(slots_per)
    edges = slots_per * block_atoms
    cube = (slots_per, block_atoms, breadth)
    readout_row = readout_ref[...].astype(f32)[None]
    couplers = (coupler_first, coupler_second)
    ee_lane = lax.broadcasted_iota(jnp.int32, (edges, breadth), 1) == 4

    def product(left, right):
        return jnp.dot(left.astype(bf16), right, preferred_element_type=f32)

    @pl.loop(0, atom_count // block_atoms)
    def _(block):
        first = pl.multiple_of(block * block_atoms, block_atoms)
        atoms = pl.ds(first, block_atoms)
        narrow = scalars[:, atoms, :]
        radial = product(narrow.reshape(edges, breadth), radial_in[...]).reshape(cube)
        paired = gathered[:, atoms, :] + source_ref[atoms, :][None] + radial
        gate = sigmoid(paired)
        value = paired * gate
        slopes = [gate + value * (1.0 - gate)]
        hidden = value.reshape(edges, breadth).astype(bf16)
        direction = [jnp.broadcast_to(narrow[:, :, k : k + 1], cube) for k in range(3)]
        smooth = jnp.broadcast_to(narrow[:, :, 3:4], cube)
        kept = []
        for layer in range(2):
            both = jnp.dot(hidden, forward_weights[layer], preferred_element_type=f32)
            carried = both[:, :breadth].reshape(cube)
            eased = smooth * carried
            environment = [
                jnp.sum(direction[k] * eased, axis=0) * norm_scale for k in range(3)
            ]
            coupled = direction[0] * environment[0][None]
            coupled = coupled + direction[1] * environment[1][None]
            coupled = coupled + direction[2] * environment[2][None]
            mixed = both[:, breadth:] + product(
                coupled.reshape(edges, breadth), couplers[layer][...]
            )
            mixed = mixed.reshape(cube)
            gate = sigmoid(mixed)
            value = mixed * gate
            slopes.append(gate + value * (1.0 - gate))
            kept.append((carried, eased, environment))
            if layer == 0:
                hidden = value.reshape(edges, breadth).astype(bf16)
        edge_energy = jnp.sum(value * readout_row, axis=2, keepdims=True)
        flow = smooth * readout_row
        sums = None
        for layer in (1, 0):
            carried, eased, environment = kept[layer]
            mixed_grad = flow * slopes[layer + 1]
            back = product(mixed_grad.reshape(edges, breadth), backward_weights[layer])
            coupled_grad = back[:, :breadth].reshape(cube)
            environment_grad = [
                jnp.sum(direction[k] * coupled_grad, axis=0) * norm_scale for k in range(3)
            ]
            spread = direction[0] * environment_grad[0][None]
            spread = spread + direction[1] * environment_grad[1][None]
            spread = spread + direction[2] * environment_grad[2][None]
            parts = [
                coupled_grad * environment[k][None] + eased * environment_grad[k][None]
                for k in range(3)
            ] + [carried * spread]
            sums = parts if sums is None else [x + y for x, y in zip(sums, parts)]
            flow = back[:, breadth:].reshape(cube) + product(
                (smooth * spread).reshape(edges, breadth), environ_turned[layer]
            ).reshape(cube)
        paired_grad = (flow * slopes[0]).reshape(edges, breadth)
        high = paired_grad.astype(bf16)
        low = (paired_grad - high.astype(f32)).astype(bf16)
        total = jnp.dot(
            jnp.concatenate([high, low], axis=1), radial_out[...], preferred_element_type=f32
        )
        total = total + jnp.dot(
            jnp.concatenate([x.reshape(edges, breadth).astype(bf16) for x in sums], axis=1),
            pick_weights[...],
            preferred_element_type=f32,
        )
        total = jnp.where(
            ee_lane, jnp.broadcast_to(edge_energy, cube).reshape(edges, breadth), total
        )
        results[:, atoms, :] = total.reshape(cube)

    scatter_ref[...] = jnp.zeros(scatter_ref.shape, f32)
    atom_ref[...] = jnp.zeros(atom_ref.shape, f32)

    @pl.loop(0, slots_per)
    def _(slot):
        flat = results[slot].T
        data = saved[slot]
        offsets = [data[k : k + 1] for k in range(3)]
        length, sine, cosine = (data[3:4], data[4:5], data[5:6])
        inverse = 1.0 / length
        scaled = length / cutoff
        under = 1.0 - scaled * scaled
        smooth = under * under
        direction = [offsets[k] * inverse for k in range(3)]
        sin_before, sin_now = (jnp.zeros_like(sine), sine)
        cos_before, cos_now = (jnp.ones_like(sine), cosine)
        first_sum = jnp.zeros_like(sine)
        second_sum = jnp.zeros_like(sine)
        for b in range(basis):
            grad = flat[8 + b : 9 + b] + flat[8 + basis + b : 9 + basis + b]
            first_sum = first_sum + grad * sin_now
            second_sum = second_sum + grad * (cos_now * ((b + 1) * math.pi / cutoff))
            sin_before, sin_now = (sin_now, 2.0 * cosine * sin_now - sin_before)
            cos_before, cos_now = (cos_now, 2.0 * cosine * cos_now - cos_before)
        edge_energy = flat[4:5]
        smooth_grad = flat[3:4] + edge_energy + first_sum * inverse
        along = flat[0:1] * direction[0] + flat[1:2] * direction[1] + flat[2:3] * direction[2]
        length_grad = smooth * inverse * (second_sum - first_sum * inverse)
        length_grad = length_grad - smooth_grad * under * (2.0 * scaled / cutoff) * 2.0
        length_grad = length_grad - along * inverse
        one_hot, in_group = chosen(slot)
        pieces = []
        atom_rows = []
        for k in range(3):
            grad = flat[k : k + 1] * inverse + length_grad * direction[k]
            atom_rows.append(-grad)
            pieces.append(jnp.where(in_group, jnp.broadcast_to(grad, in_group.shape), 0.0))
        spread = jnp.concatenate(pieces, axis=0)
        top = spread.astype(bf16)
        low = (spread - top.astype(f32)).astype(bf16)
        for piece in (top, low):
            scatter_ref[...] += lax.dot_general(
                piece, one_hot, (((1,), (1,)), ((), ())), preferred_element_type=f32
            )
        blank = jnp.zeros_like(sine)
        atom_rows = atom_rows + [edge_energy * smooth] + [blank] * 4
        atom_ref[...] += jnp.concatenate(atom_rows, axis=0)


def others(shape):
    here = (lax.axis_index("gx"), lax.axis_index("gy"))
    steps = [(n // 3 - 1, n % 3 - 1) for n in range(9)]

    def at(dx, dy):
        return (
            lax.rem(here[0] + (dx + shape[0]), shape[0]),
            lax.rem(here[1] + (dy + shape[1]), shape[1]),
        )

    return (at, steps)


def greet(shape):
    at, steps = others(shape)
    barrier = pltpu.get_barrier_semaphore()
    for dx, dy in steps:
        if (dx, dy) != (0, 0):
            pl.semaphore_signal(
                barrier, inc=1, device_id=at(dx, dy), device_id_type=pl.DeviceIdType.MESH
            )
    return barrier


def hot_columns(slots, count):
    rows = lax.broadcasted_iota(jnp.int32, (count, slots.shape[1]), 0)
    return jnp.where(rows == slots, 1.0, 0.0)


def share_kernel(
    shape,
    features,
    coords,
    slots_x,
    slots_y,
    ghosts,
    source_weight,
    target_weight,
    table_ref,
    source_ref,
    place_ref,
    own_ref,
    holding,
    leaving,
    arriving,
    ghost_rows,
    ghost_places,
    halo_rows,
    halo_places,
    move_send,
    move_recv,
    rows_send,
    rows_recv,
    places_send,
    places_recv,
):
    f32 = jnp.float32
    bf16 = jnp.bfloat16
    mesh_ids = pl.DeviceIdType.MESH
    count, breadth = features.shape
    sent = slots_x.shape[1] // 2
    ghost_count = ghosts.shape[1]
    at, steps = others(shape)
    barrier = greet(shape)

    blank = jnp.zeros((5, count), f32)
    pieces = []
    for piece in split_three(coords[...]):
        pieces += [piece, blank]
    pieces.append(jnp.zeros((breadth - 24, count), f32))
    holding[:, :breadth] = features[...]
    holding[:, breadth:] = jnp.concatenate(pieces, axis=0).T.astype(bf16)
    both = jnp.concatenate([slots_x[...], slots_y[...]], axis=1)
    picks = hot_columns(both, count).T.astype(bf16)
    ghost_hot = hot_columns(ghosts[...], count)
    ghost_picks = ghost_hot.T.astype(bf16)
    ghost_hot = ghost_hot.astype(bf16)

    for axis, slots in ((0, slots_x), (1, slots_y)):
        chosen = picks[2 * sent * axis : 2 * sent * (axis + 1)]
        payload = jnp.dot(chosen, holding[...], preferred_element_type=f32).astype(bf16)
        leaving[axis, 0] = payload[:sent]
        leaving[axis, 1] = payload[sent:]
        put = hot_columns(slots[...], count)
        hit = jnp.max(put, axis=1, keepdims=True) > 0.5
        put = put.astype(bf16)
        if axis == 0:
            pl.semaphore_wait(barrier, 8)
        copies = []
        for way, stride in ((0, 1), (1, -1)):
            copy = pltpu.make_async_remote_copy(
                src_ref=leaving.at[axis, way],
                dst_ref=arriving.at[axis, way],
                send_sem=move_send.at[axis, way],
                recv_sem=move_recv.at[axis, way],
                device_id=at(stride, 0) if axis == 0 else at(0, stride),
                device_id_type=mesh_ids,
            )
            copy.start()
            copies.append(copy)
        for copy in copies:
            copy.wait()
        came = arriving[axis].reshape(2 * sent, 2 * breadth)
        moved = jnp.dot(put, came, preferred_element_type=f32)
        holding[...] = jnp.where(hit, moved, holding[...].astype(f32)).astype(bf16)

    rows = holding[:, :breadth]
    target = jnp.dot(rows, target_weight[...], preferred_element_type=f32).astype(bf16)
    ghost_rows[...] = jnp.dot(ghost_picks, target, preferred_element_type=f32).astype(bf16)
    flat = holding[:, breadth:].astype(f32).T[:24]
    ghost_flat = jnp.dot(flat.astype(bf16), ghost_hot, preferred_element_type=f32)
    ghost_places[...] = ghost_flat[:8] + ghost_flat[8:16] + ghost_flat[16:24]
    copies = {}
    for n, (dx, dy) in enumerate(steps):
        if (dx, dy) == (0, 0):
            continue
        copies[n] = []
        for source, landing, send, recv in (
            (ghost_places, halo_places, places_send, places_recv),
            (ghost_rows, halo_rows, rows_send, rows_recv),
        ):
            copy = pltpu.make_async_remote_copy(
                src_ref=source,
                dst_ref=landing.at[n],
                send_sem=send.at[n],
                recv_sem=recv.at[n],
                device_id=at(-dx, -dy),
                device_id_type=mesh_ids,
            )
            copy.start()
            copies[n].append(copy)
    table_ref[:count, :] = target.astype(f32)
    source_ref[...] = (
        jnp.dot(rows, source_weight[...], preferred_element_type=f32).astype(bf16).astype(f32)
    )
    mine = flat[:8] + flat[8:16] + flat[16:24]
    own_ref[...] = mine
    place_ref[...] = jnp.zeros(place_ref.shape, f32)
    own_groups = count // breadth
    for k in range(3):
        for g in range(own_groups):
            place_ref[k, g : g + 1, :] = mine[k : k + 1, g * breadth : (g + 1) * breadth]
    ghost_groups = ghost_count // breadth
    for n in range(9):
        rows_at = pl.ds(count + n * ghost_count, ghost_count)
        if n not in copies:
            table_ref[rows_at, :] = jnp.zeros((ghost_count, breadth), f32)
            continue
        for copy in copies[n]:
            copy.wait()
        table_ref[rows_at, :] = halo_rows[n].astype(f32)
        places = halo_places[n]
        for k in range(3):
            for g in range(ghost_groups):
                group = own_groups + n * ghost_groups + g
                place_ref[k, group : group + 1, :] = places[
                    k : k + 1, g * breadth : (g + 1) * breadth
                ]


def return_kernel(
    shape, scattered, by_atom, ghosts, force_ref, leaving, arriving, send_sem, recv_sem
):
    f32 = jnp.float32
    bf16 = jnp.bfloat16
    count = by_atom.shape[1]
    breadth = scattered.shape[2]
    ghost_groups = ghosts.shape[1] // breadth
    own_groups = count // breadth
    at, steps = others(shape)
    barrier = greet(shape)
    blank = jnp.zeros((5, breadth), f32)
    for n in range(9):
        for g in range(ghost_groups):
            group = own_groups + n * ghost_groups + g
            piece = [scattered[k, group : group + 1, :] for k in range(3)]
            leaving[n, :, g * breadth : (g + 1) * breadth] = jnp.concatenate(
                piece + [blank], axis=0
            )
    spots = hot_columns(ghosts[...], count).T.astype(bf16)
    pl.semaphore_wait(barrier, 8)
    copies = []
    for n, (dx, dy) in enumerate(steps):
        if (dx, dy) == (0, 0):
            continue
        copy = pltpu.make_async_remote_copy(
            src_ref=leaving.at[n],
            dst_ref=arriving.at[n],
            send_sem=send_sem.at[n],
            recv_sem=recv_sem.at[n],
            device_id=at(dx, dy),
            device_id_type=pl.DeviceIdType.MESH,
        )
        copy.start()
        copies.append((n, copy))
    total = leaving[4]
    for n, copy in copies:
        copy.wait()
        total = total + arriving[n]
    stack = jnp.concatenate(split_three(total), axis=0).astype(bf16)
    back = jnp.dot(stack, spots, preferred_element_type=f32)
    back = back[:8] + back[8:16] + back[16:24]
    for k in range(3):
        own = jnp.concatenate([scattered[k, g : g + 1, :] for g in range(own_groups)], axis=1)
        force_ref[k : k + 1, :] = -(own + by_atom[k : k + 1, :] + back[k : k + 1, :])


def per_device(
    shape,
    features,
    coords,
    migrate_x_slots,
    migrate_y_slots,
    ghost_slots,
    neighbours,
    source_weight,
    target_weight,
    radial_weight,
    environ_first,
    mixing_first,
    coupler_first,
    environ_second,
    mixing_second,
    coupler_second,
    readout,
):
    features = features[0, 0]
    coords = coords[0, 0]
    neighbours = neighbours[0, 0]
    ghosts = ghost_slots.reshape(1, -1)
    count, breadth = features.shape
    slots_per = neighbours.shape[1]
    ghost_count = ghosts.shape[1]
    sent = migrate_x_slots.shape[3]
    total_rows = count + 9 * ghost_count
    groups = -(-(total_rows // breadth) // 8) * 8
    f32 = jnp.float32
    bf16 = jnp.bfloat16
    vmem = pl.BlockSpec(memory_space=pltpu.VMEM)
    smem = pl.BlockSpec(memory_space=pltpu.SMEM)
    dma = pltpu.SemaphoreType.DMA
    table, source_rows, places, own = pl.pallas_call(
        functools.partial(share_kernel, shape),
        out_shape=(
            jax.ShapeDtypeStruct((total_rows, breadth), f32),
            jax.ShapeDtypeStruct((count, breadth), f32),
            jax.ShapeDtypeStruct((3, groups, breadth), f32),
            jax.ShapeDtypeStruct((8, count), f32),
        ),
        in_specs=[vmem] * 7,
        out_specs=(vmem,) * 4,
        scratch_shapes=[
            pltpu.VMEM((count, 2 * breadth), bf16),
            pltpu.VMEM((2, 2, sent, 2 * breadth), bf16),
            pltpu.VMEM((2, 2, sent, 2 * breadth), bf16),
            pltpu.VMEM((ghost_count, breadth), bf16),
            pltpu.VMEM((8, ghost_count), f32),
            pltpu.VMEM((9, ghost_count, breadth), bf16),
            pltpu.VMEM((9, 8, ghost_count), f32),
            dma((2, 2)),
            dma((2, 2)),
            dma((9,)),
            dma((9,)),
            dma((9,)),
            dma((9,)),
        ],
        compiler_params=pltpu.CompilerParams(collective_id=0, has_side_effects=True),
        name="share",
    )(
        features,
        coords,
        migrate_x_slots.reshape(1, -1),
        migrate_y_slots.reshape(1, -1),
        ghosts,
        source_weight,
        target_weight,
    )
    by_slot = neighbours.T
    block_atoms = math.gcd(count, 16)
    cube = (slots_per, count, breadth)
    scattered, by_atom = pl.pallas_call(
        functools.partial(edge_kernel, block_atoms),
        out_shape=(
            jax.ShapeDtypeStruct((3 * groups, breadth), f32),
            jax.ShapeDtypeStruct((8, count), f32),
        ),
        in_specs=[smem] + [vmem] * 13,
        out_specs=(vmem, vmem),
        scratch_shapes=[
            pltpu.VMEM(cube, f32),
            pltpu.VMEM(cube, f32),
            pltpu.VMEM(cube, f32),
            pltpu.VMEM((slots_per, 8, count), f32),
            pltpu.VMEM((2, breadth, 2 * breadth), bf16),
            pltpu.VMEM((2, breadth, 2 * breadth), bf16),
            pltpu.VMEM((2, breadth, breadth), bf16),
            pltpu.VMEM((breadth, breadth), bf16),
            pltpu.VMEM((2 * breadth, breadth), bf16),
            pltpu.VMEM((4 * breadth, breadth), bf16),
            pltpu.VMEM((9 * groups, breadth), bf16),
        ],
        compiler_params=pltpu.CompilerParams(vmem_limit_bytes=48 * 1024 * 1024),
        name="edges",
    )(
        by_slot.reshape(-1),
        by_slot[:, None, :],
        table,
        source_rows,
        places,
        own,
        radial_weight,
        environ_first,
        mixing_first,
        coupler_first,
        environ_second,
        mixing_second,
        coupler_second,
        readout[None],
    )
    forces = pl.pallas_call(
        functools.partial(return_kernel, shape),
        out_shape=jax.ShapeDtypeStruct((3, count), f32),
        in_specs=[vmem] * 3,
        out_specs=vmem,
        scratch_shapes=[
            pltpu.VMEM((9, 8, ghost_count), f32),
            pltpu.VMEM((9, 8, ghost_count), f32),
            dma((9,)),
            dma((9,)),
        ],
        compiler_params=pltpu.CompilerParams(collective_id=1, has_side_effects=True),
        name="give_back",
    )(scattered.reshape(3, groups, breadth), by_atom, ghosts)
    return (forces[None, None], by_atom[3][None, None])


def solution(mesh):
    in_specs = (
        P("gx", "gy", None, None),
        P("gx", "gy", None, None),
        P("gx", "gy", None, None),
        P("gx", "gy", None, None),
        P("gx", "gy", None),
        P("gx", "gy", None, None),
        P(),
        P(),
        P(),
        P(),
        P(),
        P(),
        P(),
        P(),
        P(),
        P(),
    )
    out_specs = (P("gx", "gy", None, None), P("gx", "gy", None))
    return jax.shard_map(
        functools.partial(per_device, (mesh.shape["gx"], mesh.shape["gy"])),
        mesh=mesh, in_specs=in_specs, out_specs=out_specs, check_vma=False
    )
```

```python
import functools
import math

import jax
import jax.numpy as jnp
from jax import lax
from jax.experimental import pallas as pl
from jax.experimental.pallas import tpu as pltpu
from jax.sharding import PartitionSpec as P

soften = 0.25
cutoff = 2.0


def split_three(value):
    top = value.astype(jnp.bfloat16).astype(jnp.float32)
    rest = value - top
    middle = rest.astype(jnp.bfloat16).astype(jnp.float32)
    return (top, middle, rest - middle)


def sigmoid(value):
    return 0.5 * jnp.tanh(0.5 * value) + 0.5


def turned(weight):
    return weight.astype(jnp.float32).T.astype(jnp.bfloat16)


def edge_kernel(
    block_atoms,
    index_ref,
    table_ref,
    source_ref,
    place_ref,
    own_ref,
    radial_far,
    environ_first_far,
    mixing_first_far,
    coupler_first_far,
    environ_second_far,
    mixing_second_far,
    coupler_second_far,
    readout_far,
    scatter_ref,
    atom_ref,
    energy_ref,
    radial_ref,
    environ_first,
    mixing_first,
    coupler_first,
    environ_second,
    mixing_second,
    coupler_second,
    readout_ref,
    fetch_sem,
    index_sem,
    index_smem,
    gathered,
    scalars,
    results,
    saved,
    forward_weights,
    backward_weights,
    environ_turned,
    radial_in,
    radial_out,
    pick_weights,
    place_split,
):
    slots_per, atom_count = index_ref.shape
    breadth = table_ref.shape[1]
    groups = place_ref.shape[1]
    f32 = jnp.float32
    bf16 = jnp.bfloat16
    lists = [
        pltpu.make_async_copy(
            index_ref.at[slot],
            index_smem.at[pl.ds(slot * atom_count, atom_count)],
            index_sem.at[slot],
        )
        for slot in range(slots_per)
    ]
    for fetch in lists:
        fetch.start()
    fetches = [
        pltpu.make_async_copy(far, near, fetch_sem.at[n])
        for n, (far, near) in enumerate(
            (
                (radial_far, radial_ref),
                (environ_first_far, environ_first),
                (mixing_first_far, mixing_first),
                (coupler_first_far, coupler_first),
                (environ_second_far, environ_second),
                (mixing_second_far, mixing_second),
                (coupler_second_far, coupler_second),
                (readout_far, readout_ref),
            )
        )
    ]
    for fetch in fetches:
        fetch.start()

    for fetch in lists:
        fetch.wait()
    step = math.gcd(atom_count, 16)

    @pl.loop(0, slots_per)
    def _(slot):
        @pl.loop(0, atom_count // step)
        def _(part):
            base = pl.multiple_of(part * step, step)
            start = slot * atom_count + base
            for u in range(step):
                row = index_smem[start + u]
                gathered[slot, pl.ds(base + u, 1), :] = table_ref[pl.ds(row, 1), :]

    for fetch in fetches:
        fetch.wait()

    forward_weights[0, :, :breadth] = environ_first[...]
    forward_weights[0, :, breadth:] = mixing_first[...]
    forward_weights[1, :, :breadth] = environ_second[...]
    forward_weights[1, :, breadth:] = mixing_second[...]
    backward_weights[0, :, :breadth] = turned(coupler_first[...])
    backward_weights[0, :, breadth:] = turned(mixing_first[...])
    backward_weights[1, :, :breadth] = turned(coupler_second[...])
    backward_weights[1, :, breadth:] = turned(mixing_second[...])
    environ_turned[0] = turned(environ_first[...])
    environ_turned[1] = turned(environ_second[...])
    w_top, w_mid, w_low = split_three(radial_ref[...])
    basis = radial_ref.shape[0]
    lead = jnp.zeros((8, breadth), f32)
    tail = jnp.zeros((breadth - 8 - 6 * basis, breadth), f32)
    radial_in[...] = jnp.concatenate(
        [lead, w_top, w_mid, w_low, w_top, w_mid, w_top, tail], axis=0
    ).astype(bf16)
    wide = jnp.concatenate(
        [lead, w_top, w_mid, jnp.zeros((breadth - 8 - 2 * basis, breadth), f32)], axis=0
    ).T.astype(bf16)
    radial_out[:breadth, :] = wide
    radial_out[breadth:, :] = wide
    lane_id = lax.broadcasted_iota(jnp.int32, (breadth, breadth), 1)
    for k in range(4):
        pick_weights[k * breadth : (k + 1) * breadth, :] = (
            jnp.where(lane_id == k, 1.0, 0.0).astype(bf16)
        )
    places = place_ref[...].reshape(3 * groups, breadth)
    p_top, p_mid, p_low = split_three(places)
    place_split[...] = jnp.concatenate([p_top, p_mid, p_low], axis=0).astype(bf16)

    def chosen(slot):
        index = index_ref[pl.ds(slot, 1), :]
        low = lax.rem(index, breadth)
        high = lax.div(index, breadth)
        rows = lax.broadcasted_iota(jnp.int32, (breadth, atom_count), 0)
        one_hot = jnp.where(rows == low, 1.0, 0.0).astype(bf16)
        group_rows = lax.broadcasted_iota(jnp.int32, (groups, atom_count), 0)
        return (one_hot, group_rows == high)

    @pl.loop(0, slots_per, unroll=4)
    def _(slot):
        one_hot, in_group = chosen(slot)
        found = jnp.dot(place_split[...], one_hot, preferred_element_type=f32)
        size = 3 * groups
        found = found[:size] + found[size : 2 * size] + found[2 * size :]
        offsets = []
        for k in range(3):
            far = jnp.sum(
                jnp.where(in_group, found[k * groups : (k + 1) * groups], 0.0),
                axis=0,
                keepdims=True,
            )
            offsets.append(far - own_ref[k : k + 1, :])
        square = offsets[0] * offsets[0] + offsets[1] * offsets[1] + offsets[2] * offsets[2]
        length = jnp.sqrt(square + soften)
        inverse = 1.0 / length
        scaled = length / cutoff
        smooth = (1.0 - scaled * scaled) ** 2
        angle = scaled * math.pi
        sine = jnp.sin(angle)
        cosine = jnp.cos(angle)
        factor = inverse * smooth
        before, now = (jnp.zeros_like(sine), sine)
        waves = []
        for _ in range(basis):
            waves.append(now * factor)
            before, now = (now, 2.0 * cosine * now - before)
        bessel = jnp.concatenate(waves, axis=0)
        b_top, b_mid, b_low = split_three(bessel)
        blank = jnp.zeros_like(sine)
        head = [offsets[k] * inverse for k in range(3)] + [smooth] + [blank] * 4
        spare = jnp.zeros((breadth - 8 - 6 * basis, atom_count), f32)
        stack = jnp.concatenate(
            head + [b_top, b_top, b_top, b_mid, b_mid, b_low, spare], axis=0
        )
        scalars[slot] = stack.T
        saved[slot] = jnp.concatenate(offsets + [length, sine, cosine, blank, blank], axis=0)

    norm_scale = 1.0 / math.sqrt(slots_per)
    edges = slots_per * block_atoms
    cube = (slots_per, block_atoms, breadth)
    readout_row = readout_ref[...].astype(f32)[None]
    couplers = (coupler_first, coupler_second)
    ee_lane = lax.broadcasted_iota(jnp.int32, (edges, breadth), 1) == 4

    def product(left, right):
        return jnp.dot(left.astype(bf16), right, preferred_element_type=f32)

    @pl.loop(0, atom_count // block_atoms, unroll=1)
    def _(block):
        first = pl.multiple_of(block * block_atoms, block_atoms)
        atoms = pl.ds(first, block_atoms)
        narrow = scalars[:, atoms, :]
        radial = product(narrow.reshape(edges, breadth), radial_in[...]).reshape(cube)
        rows = gathered[:, atoms, :]
        paired = rows + source_ref[atoms, :][None] + radial
        gate = sigmoid(paired)
        value = paired * gate
        slopes = [gate + value * (1.0 - gate)]
        hidden = value.reshape(edges, breadth).astype(bf16)
        direction = [jnp.broadcast_to(narrow[:, :, k : k + 1], cube) for k in range(3)]
        smooth = jnp.broadcast_to(narrow[:, :, 3:4], cube)
        kept = []
        for layer in range(2):
            both = jnp.dot(hidden, forward_weights[layer], preferred_element_type=f32)
            carried = both[:, :breadth].reshape(cube)
            eased = smooth * carried
            environment = [
                jnp.sum(direction[k] * eased, axis=0) * norm_scale for k in range(3)
            ]
            coupled = direction[0] * environment[0][None]
            coupled = coupled + direction[1] * environment[1][None]
            coupled = coupled + direction[2] * environment[2][None]
            mixed = both[:, breadth:] + product(
                coupled.reshape(edges, breadth), couplers[layer][...]
            )
            mixed = mixed.reshape(cube)
            gate = sigmoid(mixed)
            value = mixed * gate
            slopes.append(gate + value * (1.0 - gate))
            kept.append((carried, eased, environment))
            if layer == 0:
                hidden = value.reshape(edges, breadth).astype(bf16)
        edge_energy = jnp.sum(value * readout_row, axis=2, keepdims=True)
        flow = smooth * readout_row
        sums = None
        for layer in (1, 0):
            carried, eased, environment = kept[layer]
            mixed_grad = flow * slopes[layer + 1]
            back = product(mixed_grad.reshape(edges, breadth), backward_weights[layer])
            coupled_grad = back[:, :breadth].reshape(cube)
            environment_grad = [
                jnp.sum(direction[k] * coupled_grad, axis=0) * norm_scale for k in range(3)
            ]
            spread = direction[0] * environment_grad[0][None]
            spread = spread + direction[1] * environment_grad[1][None]
            spread = spread + direction[2] * environment_grad[2][None]
            parts = [
                coupled_grad * environment[k][None] + eased * environment_grad[k][None]
                for k in range(3)
            ] + [carried * spread]
            sums = parts if sums is None else [x + y for x, y in zip(sums, parts)]
            flow = back[:, breadth:].reshape(cube) + product(
                (smooth * spread).reshape(edges, breadth), environ_turned[layer]
            ).reshape(cube)
        paired_grad = (flow * slopes[0]).reshape(edges, breadth)
        high = paired_grad.astype(bf16)
        low = (paired_grad - high.astype(f32)).astype(bf16)
        total = jnp.dot(
            jnp.concatenate([high, low], axis=1), radial_out[...], preferred_element_type=f32
        )
        total = total + jnp.dot(
            jnp.concatenate([x.reshape(edges, breadth).astype(bf16) for x in sums], axis=1),
            pick_weights[...],
            preferred_element_type=f32,
        )
        total = jnp.where(
            ee_lane, jnp.broadcast_to(edge_energy, cube).reshape(edges, breadth), total
        )
        results[:, atoms, :] = total.reshape(cube)

    scatter_ref[...] = jnp.zeros(scatter_ref.shape, f32)
    atom_ref[...] = jnp.zeros(atom_ref.shape, f32)
    energy_ref[...] = jnp.zeros(energy_ref.shape, f32)

    @pl.loop(0, slots_per, unroll=1)
    def _(slot):
        flat = results[slot].T
        data = saved[slot]
        offsets = [data[k : k + 1] for k in range(3)]
        length, sine, cosine = (data[3:4], data[4:5], data[5:6])
        inverse = 1.0 / length
        scaled = length / cutoff
        under = 1.0 - scaled * scaled
        smooth = under * under
        direction = [offsets[k] * inverse for k in range(3)]
        sin_before, sin_now = (jnp.zeros_like(sine), sine)
        cos_before, cos_now = (jnp.ones_like(sine), cosine)
        first_sum = jnp.zeros_like(sine)
        second_sum = jnp.zeros_like(sine)
        for b in range(basis):
            grad = flat[8 + b : 9 + b] + flat[8 + basis + b : 9 + basis + b]
            first_sum = first_sum + grad * sin_now
            second_sum = second_sum + grad * (cos_now * ((b + 1) * math.pi / cutoff))
            sin_before, sin_now = (sin_now, 2.0 * cosine * sin_now - sin_before)
            cos_before, cos_now = (cos_now, 2.0 * cosine * cos_now - cos_before)
        edge_energy = flat[4:5]
        smooth_grad = flat[3:4] + edge_energy + first_sum * inverse
        along = flat[0:1] * direction[0] + flat[1:2] * direction[1] + flat[2:3] * direction[2]
        length_grad = smooth * inverse * (second_sum - first_sum * inverse)
        length_grad = length_grad - smooth_grad * under * (2.0 * scaled / cutoff) * 2.0
        length_grad = length_grad - along * inverse
        one_hot, in_group = chosen(slot)
        pieces = []
        atom_rows = []
        for k in range(3):
            grad = flat[k : k + 1] * inverse + length_grad * direction[k]
            atom_rows.append(-grad)
            pieces.append(jnp.where(in_group, jnp.broadcast_to(grad, in_group.shape), 0.0))
        spread = jnp.concatenate(pieces, axis=0)
        top = spread.astype(bf16)
        low = (spread - top.astype(f32)).astype(bf16)
        for piece in (top, low):
            scatter_ref[...] += lax.dot_general(
                piece, one_hot, (((1,), (1,)), ((), ())), preferred_element_type=f32
            )
        blank = jnp.zeros_like(sine)
        atom_ref[...] += jnp.concatenate(atom_rows + [blank] * 5, axis=0)
        energy_ref[...] += edge_energy * smooth


def others(shape):
    here = (lax.axis_index("gx"), lax.axis_index("gy"))
    steps = [(n // 3 - 1, n % 3 - 1) for n in range(9)]

    def at(dx, dy):
        return (
            lax.rem(here[0] + (dx + shape[0]), shape[0]),
            lax.rem(here[1] + (dy + shape[1]), shape[1]),
        )

    return (at, steps)


def greet(shape):
    at, steps = others(shape)
    barrier = pltpu.get_barrier_semaphore()
    for dx, dy in steps:
        if (dx, dy) != (0, 0):
            pl.semaphore_signal(
                barrier, inc=1, device_id=at(dx, dy), device_id_type=pl.DeviceIdType.MESH
            )
    return barrier


def hot_columns(slots, count):
    rows = lax.broadcasted_iota(jnp.int32, (count, slots.shape[1]), 0)
    return jnp.where(rows == slots, 1.0, 0.0)


def share_kernel(
    shape,
    features,
    coords,
    slots_x,
    slots_y,
    ghosts,
    neighbours,
    source_weight,
    target_weight,
    table_ref,
    source_ref,
    place_ref,
    own_ref,
    index_ref,
    holding,
    leaving,
    arriving,
    ghost_rows,
    ghost_places,
    halo_rows,
    halo_places,
    move_send,
    move_recv,
    rows_send,
    rows_recv,
    places_send,
    places_recv,
):
    f32 = jnp.float32
    bf16 = jnp.bfloat16
    mesh_ids = pl.DeviceIdType.MESH
    count, breadth = features.shape
    sent = slots_x.shape[1]
    slots_per = neighbours.shape[1]
    ghost_count = ghosts.shape[1]
    at, steps = others(shape)
    barrier = greet(shape)

    blank = jnp.zeros((5, count), f32)
    pieces = []
    for piece in split_three(coords[...]):
        pieces += [piece, blank]
    pieces.append(jnp.zeros((breadth - 24, count), f32))
    holding[:, :breadth] = features[...]
    holding[:, breadth:] = jnp.concatenate(pieces, axis=0).T.astype(bf16)
    slots_x = jnp.concatenate([slots_x[0:1, :], slots_x[1:2, :]], axis=1)
    slots_y = jnp.concatenate([slots_y[0:1, :], slots_y[1:2, :]], axis=1)
    both = jnp.concatenate([slots_x, slots_y], axis=1)
    picks = hot_columns(both, count).T.astype(bf16)
    ghost_hot = hot_columns(ghosts[...], count)
    ghost_picks = ghost_hot.T.astype(bf16)
    ghost_hot = ghost_hot.astype(bf16)
    listed = neighbours[...].astype(f32)
    listed = jnp.concatenate([listed, jnp.zeros((count, breadth - slots_per), f32)], axis=1)
    index_ref[...] = listed.T[:slots_per].astype(jnp.int32)

    for axis, slots in ((0, slots_x), (1, slots_y)):
        chosen = picks[2 * sent * axis : 2 * sent * (axis + 1)]
        payload = jnp.dot(chosen, holding[...], preferred_element_type=f32).astype(bf16)
        leaving[axis, 0] = payload[:sent]
        leaving[axis, 1] = payload[sent:]
        put = hot_columns(slots, count)
        hit = jnp.max(put, axis=1, keepdims=True) > 0.5
        put = put.astype(bf16)
        if axis == 0:
            pl.semaphore_wait(barrier, 8)
        copies = []
        for way, stride in ((0, 1), (1, -1)):
            copy = pltpu.make_async_remote_copy(
                src_ref=leaving.at[axis, way],
                dst_ref=arriving.at[axis, way],
                send_sem=move_send.at[axis, way],
                recv_sem=move_recv.at[axis, way],
                device_id=at(stride, 0) if axis == 0 else at(0, stride),
                device_id_type=mesh_ids,
            )
            copy.start()
            copies.append(copy)
        for copy in copies:
            copy.wait()
        came = arriving[axis].reshape(2 * sent, 2 * breadth)
        moved = jnp.dot(put, came, preferred_element_type=f32)
        holding[...] = jnp.where(hit, moved, holding[...].astype(f32)).astype(bf16)

    rows = holding[:, :breadth]
    target = jnp.dot(rows, target_weight[...], preferred_element_type=f32).astype(bf16)
    ghost_rows[...] = jnp.dot(ghost_picks, target, preferred_element_type=f32).astype(bf16)
    flat = holding[:, breadth:].astype(f32).T[:24]
    ghost_flat = jnp.dot(flat.astype(bf16), ghost_hot, preferred_element_type=f32)
    ghost_places[...] = ghost_flat[:8] + ghost_flat[8:16] + ghost_flat[16:24]
    copies = {}
    for n, (dx, dy) in enumerate(steps):
        if (dx, dy) == (0, 0):
            continue
        copies[n] = []
        for source, landing, send, recv in (
            (ghost_places, halo_places, places_send, places_recv),
            (ghost_rows, halo_rows, rows_send, rows_recv),
        ):
            copy = pltpu.make_async_remote_copy(
                src_ref=source,
                dst_ref=landing.at[n],
                send_sem=send.at[n],
                recv_sem=recv.at[n],
                device_id=at(-dx, -dy),
                device_id_type=mesh_ids,
            )
            copy.start()
            copies[n].append(copy)
    table_ref[:count, :] = target.astype(f32)
    source_ref[...] = (
        jnp.dot(rows, source_weight[...], preferred_element_type=f32).astype(bf16).astype(f32)
    )
    mine = flat[:8] + flat[8:16] + flat[16:24]
    own_ref[...] = mine
    place_ref[...] = jnp.zeros(place_ref.shape, f32)
    own_groups = count // breadth
    for k in range(3):
        for g in range(own_groups):
            place_ref[k, g : g + 1, :] = mine[k : k + 1, g * breadth : (g + 1) * breadth]
    ghost_groups = ghost_count // breadth
    for n in range(9):
        rows_at = pl.ds(count + n * ghost_count, ghost_count)
        if n not in copies:
            table_ref[rows_at, :] = jnp.zeros((ghost_count, breadth), f32)
            continue
        for copy in copies[n]:
            copy.wait()
        table_ref[rows_at, :] = halo_rows[n].astype(f32)
        places = halo_places[n]
        for k in range(3):
            for g in range(ghost_groups):
                group = own_groups + n * ghost_groups + g
                place_ref[k, group : group + 1, :] = places[
                    k : k + 1, g * breadth : (g + 1) * breadth
                ]


def return_kernel(
    shape, scattered, by_atom, ghosts, force_ref, leaving, arriving, send_sem, recv_sem
):
    f32 = jnp.float32
    bf16 = jnp.bfloat16
    count = by_atom.shape[1]
    breadth = scattered.shape[2]
    ghost_groups = ghosts.shape[1] // breadth
    own_groups = count // breadth
    at, steps = others(shape)
    barrier = greet(shape)
    blank = jnp.zeros((5, breadth), f32)
    for n in range(9):
        for g in range(ghost_groups):
            group = own_groups + n * ghost_groups + g
            piece = [scattered[k, group : group + 1, :] for k in range(3)]
            leaving[n, :, g * breadth : (g + 1) * breadth] = jnp.concatenate(
                piece + [blank], axis=0
            )
    spots = hot_columns(ghosts[...], count).T.astype(bf16)
    pl.semaphore_wait(barrier, 8)
    copies = []
    for n, (dx, dy) in enumerate(steps):
        if (dx, dy) == (0, 0):
            continue
        copy = pltpu.make_async_remote_copy(
            src_ref=leaving.at[n],
            dst_ref=arriving.at[n],
            send_sem=send_sem.at[n],
            recv_sem=recv_sem.at[n],
            device_id=at(dx, dy),
            device_id_type=pl.DeviceIdType.MESH,
        )
        copy.start()
        copies.append((n, copy))
    total = leaving[4]
    for n, copy in copies:
        copy.wait()
        total = total + arriving[n]
    stack = jnp.concatenate(split_three(total), axis=0).astype(bf16)
    back = jnp.dot(stack, spots, preferred_element_type=f32)
    back = back[:8] + back[8:16] + back[16:24]
    for k in range(3):
        own = jnp.concatenate([scattered[k, g : g + 1, :] for g in range(own_groups)], axis=1)
        force_ref[k : k + 1, :] = -(own + by_atom[k : k + 1, :] + back[k : k + 1, :])


def per_device(
    shape,
    features,
    coords,
    migrate_x_slots,
    migrate_y_slots,
    ghost_slots,
    neighbours,
    source_weight,
    target_weight,
    radial_weight,
    environ_first,
    mixing_first,
    coupler_first,
    environ_second,
    mixing_second,
    coupler_second,
    readout,
):
    features = features[0, 0]
    coords = coords[0, 0]
    neighbours = neighbours[0, 0]
    ghosts = ghost_slots.reshape(1, -1)
    count, breadth = features.shape
    slots_per = neighbours.shape[1]
    ghost_count = ghosts.shape[1]
    sent = migrate_x_slots.shape[3]
    total_rows = count + 9 * ghost_count
    groups = -(-(total_rows // breadth) // 8) * 8
    f32 = jnp.float32
    bf16 = jnp.bfloat16
    vmem = pl.BlockSpec(memory_space=pltpu.VMEM)
    dma = pltpu.SemaphoreType.DMA
    table, source_rows, places, own, by_slot = pl.pallas_call(
        functools.partial(share_kernel, shape),
        out_shape=(
            jax.ShapeDtypeStruct((total_rows, breadth), f32),
            jax.ShapeDtypeStruct((count, breadth), f32),
            jax.ShapeDtypeStruct((3, groups, breadth), f32),
            jax.ShapeDtypeStruct((8, count), f32),
            jax.ShapeDtypeStruct((slots_per, count), jnp.int32),
        ),
        in_specs=[vmem] * 8,
        out_specs=(vmem,) * 5,
        scratch_shapes=[
            pltpu.VMEM((count, 2 * breadth), bf16),
            pltpu.VMEM((2, 2, sent, 2 * breadth), bf16),
            pltpu.VMEM((2, 2, sent, 2 * breadth), bf16),
            pltpu.VMEM((ghost_count, breadth), bf16),
            pltpu.VMEM((8, ghost_count), f32),
            pltpu.VMEM((9, ghost_count, breadth), bf16),
            pltpu.VMEM((9, 8, ghost_count), f32),
            dma((2, 2)),
            dma((2, 2)),
            dma((9,)),
            dma((9,)),
            dma((9,)),
            dma((9,)),
        ],
        compiler_params=pltpu.CompilerParams(collective_id=0, has_side_effects=True, vmem_limit_bytes=14 * 1024 * 1024
        ),
        name="share",
    )(
        features,
        coords,
        migrate_x_slots[0, 0],
        migrate_y_slots[0, 0],
        ghosts,
        neighbours,
        source_weight,
        target_weight,
    )
    block_atoms = math.gcd(count, 64)
    cube = (slots_per, count, breadth)
    scattered, by_atom, energies = pl.pallas_call(
        functools.partial(edge_kernel, block_atoms),
        out_shape=(
            jax.ShapeDtypeStruct((3 * groups, breadth), f32),
            jax.ShapeDtypeStruct((8, count), f32),
            jax.ShapeDtypeStruct((1, count), f32),
        ),
        in_specs=[vmem] * 5 + [pl.BlockSpec(memory_space=pl.ANY)] * 8,
        out_specs=(vmem,) * 3,
        scratch_shapes=[
            pltpu.VMEM(radial_weight.shape, f32),
        ]
        + [pltpu.VMEM((breadth, breadth), bf16)] * 6
        + [
            pltpu.VMEM((1, breadth), bf16),
            dma((8,)),
            dma((slots_per,)),
            pltpu.SMEM((slots_per * count,), jnp.int32),
            pltpu.VMEM(cube, f32),
            pltpu.VMEM(cube, f32),
            pltpu.VMEM(cube, f32),
            pltpu.VMEM((slots_per, 8, count), f32),
            pltpu.VMEM((2, breadth, 2 * breadth), bf16),
            pltpu.VMEM((2, breadth, 2 * breadth), bf16),
            pltpu.VMEM((2, breadth, breadth), bf16),
            pltpu.VMEM((breadth, breadth), bf16),
            pltpu.VMEM((2 * breadth, breadth), bf16),
            pltpu.VMEM((4 * breadth, breadth), bf16),
            pltpu.VMEM((9 * groups, breadth), bf16),
        ],
        compiler_params=pltpu.CompilerParams(vmem_limit_bytes=24 * 1024 * 1024),
        name="edges",
    )(
        by_slot,
        table,
        source_rows,
        places,
        own,
        radial_weight,
        environ_first,
        mixing_first,
        coupler_first,
        environ_second,
        mixing_second,
        coupler_second,
        readout[None],
    )
    forces = pl.pallas_call(
        functools.partial(return_kernel, shape),
        out_shape=jax.ShapeDtypeStruct((3, count), f32),
        in_specs=[vmem] * 3,
        out_specs=vmem,
        scratch_shapes=[
            pltpu.VMEM((9, 8, ghost_count), f32),
            pltpu.VMEM((9, 8, ghost_count), f32),
            dma((9,)),
            dma((9,)),
        ],
        compiler_params=pltpu.CompilerParams(collective_id=1, has_side_effects=True, vmem_limit_bytes=6 * 1024 * 1024
        ),
        name="give_back",
    )(scattered.reshape(3, groups, breadth), by_atom, ghosts)
    return (forces[None, None], energies[None])


def solution(mesh):
    in_specs = (
        P("gx", "gy", None, None),
        P("gx", "gy", None, None),
        P("gx", "gy", None, None),
        P("gx", "gy", None, None),
        P("gx", "gy", None),
        P("gx", "gy", None, None),
        P(),
        P(),
        P(),
        P(),
        P(),
        P(),
        P(),
        P(),
        P(),
        P(),
    )
    out_specs = (P("gx", "gy", None, None), P("gx", "gy", None))
    return jax.shard_map(
        functools.partial(per_device, (mesh.shape["gx"], mesh.shape["gy"])),
        mesh=mesh, in_specs=in_specs, out_specs=out_specs, check_vma=False
    )
```

```python
import functools
import math

import jax
import jax.numpy as jnp
from jax import lax
from jax.experimental import pallas as pl
from jax.experimental.pallas import tpu as pltpu
from jax.sharding import PartitionSpec as P

soften = 0.25
cutoff = 2.0


def split_three(value):
    top = value.astype(jnp.bfloat16).astype(jnp.float32)
    rest = value - top
    middle = rest.astype(jnp.bfloat16).astype(jnp.float32)
    return (top, middle, rest - middle)


def sigmoid(value):
    return 0.5 * jnp.tanh(0.5 * value) + 0.5


def turned(weight):
    return weight.astype(jnp.float32).T.astype(jnp.bfloat16)


def edge_kernel(
    block_atoms,
    index_ref,
    table_ref,
    source_ref,
    place_ref,
    own_ref,
    radial_far,
    environ_first_far,
    mixing_first_far,
    coupler_first_far,
    environ_second_far,
    mixing_second_far,
    coupler_second_far,
    readout_far,
    scatter_ref,
    atom_ref,
    energy_ref,
    radial_ref,
    environ_first,
    mixing_first,
    coupler_first,
    environ_second,
    mixing_second,
    coupler_second,
    readout_ref,
    fetch_sem,
    index_sem,
    index_smem,
    gathered,
    scalars,
    results,
    saved,
    forward_weights,
    backward_weights,
    environ_turned,
    radial_in,
    radial_out,
    pick_weights,
    place_split,
):
    slots_per, atom_count = index_ref.shape
    breadth = table_ref.shape[1]
    groups = place_ref.shape[1]
    f32 = jnp.float32
    bf16 = jnp.bfloat16
    lists = [
        pltpu.make_async_copy(
            index_ref.at[slot],
            index_smem.at[pl.ds(slot * atom_count, atom_count)],
            index_sem.at[slot],
        )
        for slot in range(slots_per)
    ]
    for fetch in lists:
        fetch.start()
    fetches = [
        pltpu.make_async_copy(far, near, fetch_sem.at[n])
        for n, (far, near) in enumerate(
            (
                (radial_far, radial_ref),
                (environ_first_far, environ_first),
                (mixing_first_far, mixing_first),
                (coupler_first_far, coupler_first),
                (environ_second_far, environ_second),
                (mixing_second_far, mixing_second),
                (coupler_second_far, coupler_second),
                (readout_far, readout_ref),
            )
        )
    ]
    for fetch in fetches:
        fetch.start()

    for fetch in lists:
        fetch.wait()
    step = math.gcd(atom_count, 16)

    @pl.loop(0, slots_per)
    def _(slot):
        @pl.loop(0, atom_count // step)
        def _(part):
            base = pl.multiple_of(part * step, step)
            start = slot * atom_count + base
            for u in range(step):
                row = index_smem[start + u]
                gathered[slot, pl.ds(base + u, 1), :] = table_ref[pl.ds(row, 1), :]

    for fetch in fetches:
        fetch.wait()

    forward_weights[0, :, :breadth] = environ_first[...]
    forward_weights[0, :, breadth:] = mixing_first[...]
    forward_weights[1, :, :breadth] = environ_second[...]
    forward_weights[1, :, breadth:] = mixing_second[...]
    backward_weights[0, :, :breadth] = turned(coupler_first[...])
    backward_weights[0, :, breadth:] = turned(mixing_first[...])
    backward_weights[1, :, :breadth] = turned(coupler_second[...])
    backward_weights[1, :, breadth:] = turned(mixing_second[...])
    environ_turned[0] = turned(environ_first[...])
    environ_turned[1] = turned(environ_second[...])
    w_top, w_mid, w_low = split_three(radial_ref[...])
    basis = radial_ref.shape[0]
    lead = jnp.zeros((8, breadth), f32)
    tail = jnp.zeros((breadth - 8 - 6 * basis, breadth), f32)
    radial_in[...] = jnp.concatenate(
        [lead, w_top, w_mid, w_low, w_top, w_mid, w_top, tail], axis=0
    ).astype(bf16)
    wide = jnp.concatenate(
        [lead, w_top, w_mid, jnp.zeros((breadth - 8 - 2 * basis, breadth), f32)], axis=0
    ).T.astype(bf16)
    radial_out[:breadth, :] = wide
    radial_out[breadth:, :] = wide
    lane_id = lax.broadcasted_iota(jnp.int32, (breadth, breadth), 1)
    for k in range(4):
        pick_weights[k * breadth : (k + 1) * breadth, :] = (
            jnp.where(lane_id == k, 1.0, 0.0).astype(bf16)
        )
    places = place_ref[...].reshape(3 * groups, breadth)
    p_top, p_mid, p_low = split_three(places)
    place_split[...] = jnp.concatenate([p_top, p_mid, p_low], axis=0).astype(bf16)

    def chosen(slot):
        index = index_ref[pl.ds(slot, 1), :]
        low = lax.rem(index, breadth)
        high = lax.div(index, breadth)
        rows = lax.broadcasted_iota(jnp.int32, (breadth, atom_count), 0)
        one_hot = jnp.where(rows == low, 1.0, 0.0).astype(bf16)
        group_rows = lax.broadcasted_iota(jnp.int32, (groups, atom_count), 0)
        return (one_hot, group_rows == high)

    @pl.loop(0, slots_per, unroll=4)
    def _(slot):
        one_hot, in_group = chosen(slot)
        found = jnp.dot(place_split[...], one_hot, preferred_element_type=f32)
        size = 3 * groups
        found = found[:size] + found[size : 2 * size] + found[2 * size :]
        offsets = []
        for k in range(3):
            far = jnp.sum(
                jnp.where(in_group, found[k * groups : (k + 1) * groups], 0.0),
                axis=0,
                keepdims=True,
            )
            offsets.append(far - own_ref[k : k + 1, :])
        square = offsets[0] * offsets[0] + offsets[1] * offsets[1] + offsets[2] * offsets[2]
        length = jnp.sqrt(square + soften)
        inverse = 1.0 / length
        scaled = length / cutoff
        smooth = (1.0 - scaled * scaled) ** 2
        angle = scaled * math.pi
        sine = jnp.sin(angle)
        cosine = jnp.cos(angle)
        factor = inverse * smooth
        before, now = (jnp.zeros_like(sine), sine)
        waves = []
        for _ in range(basis):
            waves.append(now * factor)
            before, now = (now, 2.0 * cosine * now - before)
        bessel = jnp.concatenate(waves, axis=0)
        b_top, b_mid, b_low = split_three(bessel)
        blank = jnp.zeros_like(sine)
        head = [offsets[k] * inverse for k in range(3)] + [smooth] + [blank] * 4
        spare = jnp.zeros((breadth - 8 - 6 * basis, atom_count), f32)
        stack = jnp.concatenate(
            head + [b_top, b_top, b_top, b_mid, b_mid, b_low, spare], axis=0
        )
        scalars[slot] = stack.T
        saved[slot] = jnp.concatenate(offsets + [length, sine, cosine, blank, blank], axis=0)

    norm_scale = 1.0 / math.sqrt(slots_per)
    edges = slots_per * block_atoms
    cube = (slots_per, block_atoms, breadth)
    readout_row = readout_ref[...].astype(f32)[None]
    couplers = (coupler_first, coupler_second)
    ee_lane = lax.broadcasted_iota(jnp.int32, (edges, breadth), 1) == 4

    def product(left, right):
        return jnp.dot(left.astype(bf16), right, preferred_element_type=f32)

    @pl.loop(0, atom_count // block_atoms, unroll=1)
    def _(block):
        first = pl.multiple_of(block * block_atoms, block_atoms)
        atoms = pl.ds(first, block_atoms)
        narrow = scalars[:, atoms, :]
        radial = product(narrow.reshape(edges, breadth), radial_in[...]).reshape(cube)
        rows = gathered[:, atoms, :]
        paired = rows + source_ref[atoms, :][None] + radial
        gate = sigmoid(paired)
        value = paired * gate
        slopes = [gate + value * (1.0 - gate)]
        hidden = value.reshape(edges, breadth).astype(bf16)
        direction = [jnp.broadcast_to(narrow[:, :, k : k + 1], cube) for k in range(3)]
        smooth = jnp.broadcast_to(narrow[:, :, 3:4], cube)
        kept = []
        for layer in range(2):
            both = jnp.dot(hidden, forward_weights[layer], preferred_element_type=f32)
            carried = both[:, :breadth].reshape(cube)
            eased = smooth * carried
            environment = [
                jnp.sum(direction[k] * eased, axis=0) * norm_scale for k in range(3)
            ]
            coupled = direction[0] * environment[0][None]
            coupled = coupled + direction[1] * environment[1][None]
            coupled = coupled + direction[2] * environment[2][None]
            mixed = both[:, breadth:] + product(
                coupled.reshape(edges, breadth), couplers[layer][...]
            )
            mixed = mixed.reshape(cube)
            gate = sigmoid(mixed)
            value = mixed * gate
            slopes.append(gate + value * (1.0 - gate))
            kept.append((carried, eased, environment))
            if layer == 0:
                hidden = value.reshape(edges, breadth).astype(bf16)
        edge_energy = jnp.sum(value * readout_row, axis=2, keepdims=True)
        flow = smooth * readout_row
        sums = None
        for layer in (1, 0):
            carried, eased, environment = kept[layer]
            mixed_grad = flow * slopes[layer + 1]
            back = product(mixed_grad.reshape(edges, breadth), backward_weights[layer])
            coupled_grad = back[:, :breadth].reshape(cube)
            environment_grad = [
                jnp.sum(direction[k] * coupled_grad, axis=0) * norm_scale for k in range(3)
            ]
            spread = direction[0] * environment_grad[0][None]
            spread = spread + direction[1] * environment_grad[1][None]
            spread = spread + direction[2] * environment_grad[2][None]
            parts = [
                coupled_grad * environment[k][None] + eased * environment_grad[k][None]
                for k in range(3)
            ] + [carried * spread]
            sums = parts if sums is None else [x + y for x, y in zip(sums, parts)]
            flow = back[:, breadth:].reshape(cube) + product(
                (smooth * spread).reshape(edges, breadth), environ_turned[layer]
            ).reshape(cube)
        paired_grad = (flow * slopes[0]).reshape(edges, breadth)
        high = paired_grad.astype(bf16)
        low = (paired_grad - high.astype(f32)).astype(bf16)
        total = jnp.dot(
            jnp.concatenate([high, low], axis=1), radial_out[...], preferred_element_type=f32
        )
        total = total + jnp.dot(
            jnp.concatenate([x.reshape(edges, breadth).astype(bf16) for x in sums], axis=1),
            pick_weights[...],
            preferred_element_type=f32,
        )
        total = jnp.where(
            ee_lane, jnp.broadcast_to(edge_energy, cube).reshape(edges, breadth), total
        )
        results[:, atoms, :] = total.reshape(cube)

    scatter_ref[...] = jnp.zeros(scatter_ref.shape, f32)
    atom_ref[...] = jnp.zeros(atom_ref.shape, f32)
    energy_ref[...] = jnp.zeros(energy_ref.shape, f32)

    @pl.loop(0, slots_per, unroll=1)
    def _(slot):
        flat = results[slot].T
        data = saved[slot]
        offsets = [data[k : k + 1] for k in range(3)]
        length, sine, cosine = (data[3:4], data[4:5], data[5:6])
        inverse = 1.0 / length
        scaled = length / cutoff
        under = 1.0 - scaled * scaled
        smooth = under * under
        direction = [offsets[k] * inverse for k in range(3)]
        sin_before, sin_now = (jnp.zeros_like(sine), sine)
        cos_before, cos_now = (jnp.ones_like(sine), cosine)
        first_sum = jnp.zeros_like(sine)
        second_sum = jnp.zeros_like(sine)
        for b in range(basis):
            grad = flat[8 + b : 9 + b] + flat[8 + basis + b : 9 + basis + b]
            first_sum = first_sum + grad * sin_now
            second_sum = second_sum + grad * (cos_now * ((b + 1) * math.pi / cutoff))
            sin_before, sin_now = (sin_now, 2.0 * cosine * sin_now - sin_before)
            cos_before, cos_now = (cos_now, 2.0 * cosine * cos_now - cos_before)
        edge_energy = flat[4:5]
        smooth_grad = flat[3:4] + edge_energy + first_sum * inverse
        along = flat[0:1] * direction[0] + flat[1:2] * direction[1] + flat[2:3] * direction[2]
        length_grad = smooth * inverse * (second_sum - first_sum * inverse)
        length_grad = length_grad - smooth_grad * under * (2.0 * scaled / cutoff) * 2.0
        length_grad = length_grad - along * inverse
        one_hot, in_group = chosen(slot)
        pieces = []
        atom_rows = []
        for k in range(3):
            grad = flat[k : k + 1] * inverse + length_grad * direction[k]
            atom_rows.append(-grad)
            pieces.append(jnp.where(in_group, jnp.broadcast_to(grad, in_group.shape), 0.0))
        spread = jnp.concatenate(pieces, axis=0)
        top = spread.astype(bf16)
        low = (spread - top.astype(f32)).astype(bf16)
        for piece in (top, low):
            scatter_ref[...] += lax.dot_general(
                piece, one_hot, (((1,), (1,)), ((), ())), preferred_element_type=f32
            )
        blank = jnp.zeros_like(sine)
        atom_ref[...] += jnp.concatenate(atom_rows + [blank] * 5, axis=0)
        energy_ref[...] += edge_energy * smooth


def others(shape):
    here = (lax.axis_index("gx"), lax.axis_index("gy"))
    steps = [(n // 3 - 1, n % 3 - 1) for n in range(9)]

    def at(dx, dy):
        return (
            lax.rem(here[0] + (dx + shape[0]), shape[0]),
            lax.rem(here[1] + (dy + shape[1]), shape[1]),
        )

    return (at, steps)


def greet(shape):
    at, steps = others(shape)
    barrier = pltpu.get_barrier_semaphore()
    for dx, dy in steps:
        if (dx, dy) != (0, 0):
            pl.semaphore_signal(
                barrier, inc=1, device_id=at(dx, dy), device_id_type=pl.DeviceIdType.MESH
            )
    return barrier


def hot_columns(slots, count):
    rows = lax.broadcasted_iota(jnp.int32, (count, slots.shape[1]), 0)
    return jnp.where(rows == slots, 1.0, 0.0)


def share_kernel(
    shape,
    features_far,
    coords,
    slots_x_far,
    slots_y_far,
    ghosts_far,
    neighbours,
    source_weight_far,
    target_weight_far,
    table_ref,
    source_ref,
    place_ref,
    own_ref,
    index_ref,
    features,
    slots_x,
    slots_y,
    ghosts,
    source_weight,
    target_weight,
    fetch_sem,
    holding,
    leaving,
    arriving,
    ghost_rows,
    ghost_places,
    halo_rows,
    halo_places,
    move_send,
    move_recv,
    rows_send,
    rows_recv,
    places_send,
    places_recv,
):
    f32 = jnp.float32
    bf16 = jnp.bfloat16
    mesh_ids = pl.DeviceIdType.MESH
    count, breadth = features.shape
    sent = slots_x.shape[1]
    slots_per = neighbours.shape[1]
    ghost_count = ghosts.shape[1]
    at, steps = others(shape)
    barrier = greet(shape)
    fetches = [
        pltpu.make_async_copy(far, near, fetch_sem.at[n])
        for n, (far, near) in enumerate(
            (
                (features_far, features),
                (slots_x_far, slots_x),
                (slots_y_far, slots_y),
                (ghosts_far, ghosts),
                (source_weight_far, source_weight),
                (target_weight_far, target_weight),
            )
        )
    ]
    for fetch in fetches:
        fetch.start()

    blank = jnp.zeros((5, count), f32)
    pieces = []
    for piece in split_three(coords[...]):
        pieces += [piece, blank]
    pieces.append(jnp.zeros((breadth - 24, count), f32))
    holding[:, breadth:] = jnp.concatenate(pieces, axis=0).T.astype(bf16)
    for fetch in fetches:
        fetch.wait()
    holding[:, :breadth] = features[...]
    slots_x = jnp.concatenate([slots_x[0:1, :], slots_x[1:2, :]], axis=1)
    slots_y = jnp.concatenate([slots_y[0:1, :], slots_y[1:2, :]], axis=1)
    both = jnp.concatenate([slots_x, slots_y], axis=1)
    picks = hot_columns(both, count).T.astype(bf16)
    ghost_hot = hot_columns(ghosts[...], count)
    ghost_picks = ghost_hot.T.astype(bf16)
    ghost_hot = ghost_hot.astype(bf16)
    listed = neighbours[...].astype(f32)
    listed = jnp.concatenate([listed, jnp.zeros((count, breadth - slots_per), f32)], axis=1)
    index_ref[...] = listed.T[:slots_per].astype(jnp.int32)

    for axis, slots in ((0, slots_x), (1, slots_y)):
        chosen = picks[2 * sent * axis : 2 * sent * (axis + 1)]
        payload = jnp.dot(chosen, holding[...], preferred_element_type=f32).astype(bf16)
        leaving[axis, 0] = payload[:sent]
        leaving[axis, 1] = payload[sent:]
        put = hot_columns(slots, count)
        hit = jnp.max(put, axis=1, keepdims=True) > 0.5
        put = put.astype(bf16)
        if axis == 0:
            pl.semaphore_wait(barrier, 8)
        copies = []
        for way, stride in ((0, 1), (1, -1)):
            copy = pltpu.make_async_remote_copy(
                src_ref=leaving.at[axis, way],
                dst_ref=arriving.at[axis, way],
                send_sem=move_send.at[axis, way],
                recv_sem=move_recv.at[axis, way],
                device_id=at(stride, 0) if axis == 0 else at(0, stride),
                device_id_type=mesh_ids,
            )
            copy.start()
            copies.append(copy)
        for copy in copies:
            copy.wait()
        came = arriving[axis].reshape(2 * sent, 2 * breadth)
        moved = jnp.dot(put, came, preferred_element_type=f32)
        holding[...] = jnp.where(hit, moved, holding[...].astype(f32)).astype(bf16)

    rows = holding[:, :breadth]
    target = jnp.dot(rows, target_weight[...], preferred_element_type=f32).astype(bf16)
    ghost_rows[...] = jnp.dot(ghost_picks, target, preferred_element_type=f32).astype(bf16)
    flat = holding[:, breadth:].astype(f32).T[:24]
    ghost_flat = jnp.dot(flat.astype(bf16), ghost_hot, preferred_element_type=f32)
    ghost_places[...] = ghost_flat[:8] + ghost_flat[8:16] + ghost_flat[16:24]
    copies = {}
    for n, (dx, dy) in enumerate(steps):
        if (dx, dy) == (0, 0):
            continue
        copies[n] = []
        for source, landing, send, recv in (
            (ghost_places, halo_places, places_send, places_recv),
            (ghost_rows, halo_rows, rows_send, rows_recv),
        ):
            copy = pltpu.make_async_remote_copy(
                src_ref=source,
                dst_ref=landing.at[n],
                send_sem=send.at[n],
                recv_sem=recv.at[n],
                device_id=at(-dx, -dy),
                device_id_type=mesh_ids,
            )
            copy.start()
            copies[n].append(copy)
    table_ref[:count, :] = target.astype(f32)
    source_ref[...] = (
        jnp.dot(rows, source_weight[...], preferred_element_type=f32).astype(bf16).astype(f32)
    )
    mine = flat[:8] + flat[8:16] + flat[16:24]
    own_ref[...] = mine
    place_ref[...] = jnp.zeros(place_ref.shape, f32)
    own_groups = count // breadth
    for k in range(3):
        for g in range(own_groups):
            place_ref[k, g : g + 1, :] = mine[k : k + 1, g * breadth : (g + 1) * breadth]
    ghost_groups = ghost_count // breadth
    for n in range(9):
        rows_at = pl.ds(count + n * ghost_count, ghost_count)
        if n not in copies:
            table_ref[rows_at, :] = jnp.zeros((ghost_count, breadth), f32)
            continue
        for copy in copies[n]:
            copy.wait()
        table_ref[rows_at, :] = halo_rows[n].astype(f32)
        places = halo_places[n]
        for k in range(3):
            for g in range(ghost_groups):
                group = own_groups + n * ghost_groups + g
                place_ref[k, group : group + 1, :] = places[
                    k : k + 1, g * breadth : (g + 1) * breadth
                ]


def return_kernel(
    shape, scattered, by_atom, ghosts, force_ref, leaving, arriving, send_sem, recv_sem
):
    f32 = jnp.float32
    bf16 = jnp.bfloat16
    count = by_atom.shape[1]
    breadth = scattered.shape[2]
    ghost_groups = ghosts.shape[1] // breadth
    own_groups = count // breadth
    at, steps = others(shape)
    barrier = greet(shape)
    blank = jnp.zeros((5, breadth), f32)
    for n in range(9):
        for g in range(ghost_groups):
            group = own_groups + n * ghost_groups + g
            piece = [scattered[k, group : group + 1, :] for k in range(3)]
            leaving[n, :, g * breadth : (g + 1) * breadth] = jnp.concatenate(
                piece + [blank], axis=0
            )
    spots = hot_columns(ghosts[...], count).T.astype(bf16)
    pl.semaphore_wait(barrier, 8)
    copies = []
    for n, (dx, dy) in enumerate(steps):
        if (dx, dy) == (0, 0):
            continue
        copy = pltpu.make_async_remote_copy(
            src_ref=leaving.at[n],
            dst_ref=arriving.at[n],
            send_sem=send_sem.at[n],
            recv_sem=recv_sem.at[n],
            device_id=at(dx, dy),
            device_id_type=pl.DeviceIdType.MESH,
        )
        copy.start()
        copies.append((n, copy))
    total = leaving[4]
    for n, copy in copies:
        copy.wait()
        total = total + arriving[n]
    stack = jnp.concatenate(split_three(total), axis=0).astype(bf16)
    back = jnp.dot(stack, spots, preferred_element_type=f32)
    back = back[:8] + back[8:16] + back[16:24]
    for k in range(3):
        own = jnp.concatenate([scattered[k, g : g + 1, :] for g in range(own_groups)], axis=1)
        force_ref[k : k + 1, :] = -(own + by_atom[k : k + 1, :] + back[k : k + 1, :])


def per_device(
    shape,
    features,
    coords,
    migrate_x_slots,
    migrate_y_slots,
    ghost_slots,
    neighbours,
    source_weight,
    target_weight,
    radial_weight,
    environ_first,
    mixing_first,
    coupler_first,
    environ_second,
    mixing_second,
    coupler_second,
    readout,
):
    features = features[0, 0]
    coords = coords[0, 0]
    neighbours = neighbours[0, 0]
    ghosts = ghost_slots.reshape(1, -1)
    count, breadth = features.shape
    slots_per = neighbours.shape[1]
    ghost_count = ghosts.shape[1]
    sent = migrate_x_slots.shape[3]
    total_rows = count + 9 * ghost_count
    groups = -(-(total_rows // breadth) // 8) * 8
    f32 = jnp.float32
    bf16 = jnp.bfloat16
    vmem = pl.BlockSpec(memory_space=pltpu.VMEM)
    hbm = pl.BlockSpec(memory_space=pltpu.HBM)
    dma = pltpu.SemaphoreType.DMA
    table, source_rows, places, own, by_slot = pl.pallas_call(
        functools.partial(share_kernel, shape),
        out_shape=(
            jax.ShapeDtypeStruct((total_rows, breadth), f32),
            jax.ShapeDtypeStruct((count, breadth), f32),
            jax.ShapeDtypeStruct((3, groups, breadth), f32),
            jax.ShapeDtypeStruct((8, count), f32),
            jax.ShapeDtypeStruct((slots_per, count), jnp.int32),
        ),
        in_specs=[hbm, vmem, hbm, hbm, hbm, vmem, hbm, hbm],
        out_specs=(vmem,) * 5,
        scratch_shapes=[
            pltpu.VMEM((count, breadth), bf16),
            pltpu.VMEM((2, sent), jnp.int32),
            pltpu.VMEM((2, sent), jnp.int32),
            pltpu.VMEM((1, ghost_count), jnp.int32),
            pltpu.VMEM((breadth, breadth), bf16),
            pltpu.VMEM((breadth, breadth), bf16),
            dma((6,)),
            pltpu.VMEM((count, 2 * breadth), bf16),
            pltpu.VMEM((2, 2, sent, 2 * breadth), bf16),
            pltpu.VMEM((2, 2, sent, 2 * breadth), bf16),
            pltpu.VMEM((ghost_count, breadth), bf16),
            pltpu.VMEM((8, ghost_count), f32),
            pltpu.VMEM((9, ghost_count, breadth), bf16),
            pltpu.VMEM((9, 8, ghost_count), f32),
            dma((2, 2)),
            dma((2, 2)),
            dma((9,)),
            dma((9,)),
            dma((9,)),
            dma((9,)),
        ],
        compiler_params=pltpu.CompilerParams(collective_id=0, has_side_effects=True, vmem_limit_bytes=67043328
        ),
        name="share",
    )(
        features,
        coords,
        migrate_x_slots[0, 0],
        migrate_y_slots[0, 0],
        ghosts,
        neighbours,
        source_weight,
        target_weight,
    )
    block_atoms = math.gcd(count, 64)
    cube = (slots_per, count, breadth)
    scattered, by_atom, energies = pl.pallas_call(
        functools.partial(edge_kernel, block_atoms),
        out_shape=(
            jax.ShapeDtypeStruct((3 * groups, breadth), f32),
            jax.ShapeDtypeStruct((8, count), f32),
            jax.ShapeDtypeStruct((1, count), f32),
        ),
        in_specs=[vmem] * 5 + [pl.BlockSpec(memory_space=pltpu.HBM)] * 8,
        out_specs=(vmem,) * 3,
        scratch_shapes=[
            pltpu.VMEM(radial_weight.shape, f32),
        ]
        + [pltpu.VMEM((breadth, breadth), bf16)] * 6
        + [
            pltpu.VMEM((1, breadth), bf16),
            dma((8,)),
            dma((slots_per,)),
            pltpu.SMEM((slots_per * count,), jnp.int32),
            pltpu.VMEM(cube, f32),
            pltpu.VMEM(cube, f32),
            pltpu.VMEM(cube, f32),
            pltpu.VMEM((slots_per, 8, count), f32),
            pltpu.VMEM((2, breadth, 2 * breadth), bf16),
            pltpu.VMEM((2, breadth, 2 * breadth), bf16),
            pltpu.VMEM((2, breadth, breadth), bf16),
            pltpu.VMEM((breadth, breadth), bf16),
            pltpu.VMEM((2 * breadth, breadth), bf16),
            pltpu.VMEM((4 * breadth, breadth), bf16),
            pltpu.VMEM((9 * groups, breadth), bf16),
        ],
        compiler_params=pltpu.CompilerParams(vmem_limit_bytes=67043328),
        name="edges",
    )(
        by_slot,
        table,
        source_rows,
        places,
        own,
        radial_weight,
        environ_first,
        mixing_first,
        coupler_first,
        environ_second,
        mixing_second,
        coupler_second,
        readout[None],
    )
    forces = pl.pallas_call(
        functools.partial(return_kernel, shape),
        out_shape=jax.ShapeDtypeStruct((3, count), f32),
        in_specs=[vmem] * 3,
        out_specs=vmem,
        scratch_shapes=[
            pltpu.VMEM((9, 8, ghost_count), f32),
            pltpu.VMEM((9, 8, ghost_count), f32),
            dma((9,)),
            dma((9,)),
        ],
        compiler_params=pltpu.CompilerParams(collective_id=1, has_side_effects=True, vmem_limit_bytes=67043328
        ),
        name="give_back",
    )(scattered.reshape(3, groups, breadth), by_atom, ghosts)
    return (forces[None, None], energies[None])


def solution(mesh):
    in_specs = (
        P("gx", "gy", None, None),
        P("gx", "gy", None, None),
        P("gx", "gy", None, None),
        P("gx", "gy", None, None),
        P("gx", "gy", None),
        P("gx", "gy", None, None),
        P(),
        P(),
        P(),
        P(),
        P(),
        P(),
        P(),
        P(),
        P(),
        P(),
    )
    out_specs = (P("gx", "gy", None, None), P("gx", "gy", None))
    return jax.shard_map(
        functools.partial(per_device, (mesh.shape["gx"], mesh.shape["gy"])),
        mesh=mesh, in_specs=in_specs, out_specs=out_specs, check_vma=False
    )
```
